32 devices in a mesh: groups: 1, row: 16 (over z, y, core), col: 2 (over x), rep: 1.
Axes of the slice: x: 2, y: 2, z: 4, core: 2. Of those that a mesh axis runs over, the one named last changes fastest.
Arguments:
- bins: bfloat16 [256, 1536], P(('groups', 'row', 'col')), may hold values from -6 to 6
- row_proj: bfloat16 [96, 1536], P('rep'), may hold values from -0.15625 to 0.15625
- col_proj: bfloat16 [96, 1536], P('rep'), may hold values from -0.15625 to 0.15625
- conv_weight: bfloat16 [3, 9, 96, 96], P(None, None, 'rep'), may hold values from -0.21875 to 0.21875
- conv_bias: float32 [3, 96], P(None, 'rep'), may hold values from -3 to 3
Outputs:
- contact_map: bfloat16 [96, 256, 256], P('rep', ('groups', 'row'), 'col')
The draws below stay inside these ranges and needn't reach their ends.
All inputs are finite; a program needn't handle non-finite values.
Results may differ from the reference program's by a relative error of at most 0.013.
Values may be sent and summed in bfloat16 or wider, within the bound.
No kernel may reach another device: no remote copies, remote signals or barrier semaphores. Data moves between devices by JAX's collectives and lax.ppermute only.
A program may use at most 128 MiB of HBM per device.

```python
import jax
import jax.numpy as jnp
from jax import lax

E = 1536
C = 96
LAYERS = 3
BINS = 256


def level_of(stream_key, shape, shards, low, high):
    loudness, own = 1.0, jax.random.fold_in(stream_key, 6)
    for position, parts in shards:
        steps = jnp.exp(jax.random.uniform(jax.random.fold_in(own, position), (parts,), jnp.float32, low / len(shards), high / len(shards)))
        loudness = loudness * jnp.repeat(steps, shape[position] // parts).reshape([-1 if axis == position else 1 for axis in range(len(shape))])
    return loudness


def bell_draw(own_key, dims, width, bound, shards=(), held_as=jnp.bfloat16):
    factor_of = level_of(own_key, dims, shards, -0.22, 0.18) if shards else 1.0
    array = jax.random.normal(own_key, dims, jnp.float32) * width * factor_of
    return jnp.minimum(jnp.maximum(array, -bound), bound).astype(held_as)


def setup_inputs(seed: int = 0, part: int = 0) -> dict:
    key_list = jax.random.split(jax.random.key(seed), 6)
    own_keys = jax.random.split(jax.random.fold_in(key_list[5], part), 6)
    bins = bell_draw(own_keys[0], (BINS, E), 1.0, 6.0, ((0, 32),))
    row_proj = bell_draw(key_list[1], (C, E), E ** -0.5, 0.15625)
    col_proj = bell_draw(key_list[2], (C, E), E ** -0.5, 0.15625)
    conv_weight = bell_draw(key_list[3], (LAYERS, 9, C, C), (9 * C) ** -0.5, 0.21875)
    conv_bias = bell_draw(key_list[4], (LAYERS, C), 0.5, 3.0, (), jnp.float32)
    return dict(bins=bins, row_proj=row_proj, col_proj=col_proj, conv_weight=conv_weight, conv_bias=conv_bias)


def conv_layer(state, weights, bias, spread):
    active = jnp.maximum(state, 0).astype(jnp.float32)[None]
    channels_out = weights.shape[1]
    channels_in = weights.shape[2]
    kernel = weights.astype(jnp.float32).reshape(3, 3, channels_out, channels_in).transpose(2, 3, 0, 1)
    conv = lax.conv_general_dilated(active, kernel, (1, 1), [(spread, spread), (spread, spread)], rhs_dilation=(spread, spread), dimension_numbers=("NCHW", "OIHW", "NCHW"), precision=lax.Precision.HIGHEST)[0]
    return (state.astype(jnp.float32) + conv + bias.astype(jnp.float32)[:, None, None]).astype(jnp.bfloat16)


def reference(bins, row_proj, col_proj, conv_weight, conv_bias):
    row_terms = jnp.dot(bins, row_proj.T, preferred_element_type=jnp.float32).astype(jnp.bfloat16)
    col_terms = jnp.dot(bins, col_proj.T, preferred_element_type=jnp.float32).astype(jnp.bfloat16)
    state = (row_terms.T.astype(jnp.float32)[:, :, None] * col_terms.T.astype(jnp.float32)[:, None, :]).astype(jnp.bfloat16)
    state = conv_layer(state, conv_weight[0], conv_bias[0], 1)
    state = conv_layer(state, conv_weight[1], conv_bias[1], 2)
    widened = state.astype(jnp.float32)
    state = ((widened + widened.transpose(0, 2, 1)) * 0.5).astype(jnp.bfloat16)
    state = conv_layer(state, conv_weight[2], conv_bias[2], 4)
    return state
```

```python
import functools
import jax
import jax.numpy as jnp
from jax import lax
from jax.experimental import pallas as pl
from jax.experimental.pallas import tpu as pltpu
from jax.sharding import PartitionSpec as P

LANES = 128
PAD = 16
NT = (((1,), (1,)), ((), ()))


def pick(count, most):
    return max(k for k in range(1, min(count, most) + 1) if count % k == 0)


def decoder_kernel(tr, tc, terms_ref, w_ref, bias_ref, out_ref,
                   rows_f, cols_f, vtab, utab, w0, w1, w2, h1, sym, acc):
    bins = terms_ref.shape[0]
    ch = w_ref.shape[2]
    wide = tc + 16
    span = tc + 8
    i0 = lax.axis_index("row") * tr
    j0 = lax.axis_index("col") * tc
    f32, bf16 = jnp.float32, jnp.bfloat16

    for tab, lo in ((rows_f, 0), (cols_f, LANES)):
        tab[0:PAD] = jnp.zeros((PAD, LANES), f32)
        tab[PAD + bins:] = jnp.zeros((PAD, LANES), f32)
        tab[PAD:PAD + bins] = terms_ref[:, lo:lo + LANES].astype(f32)

    w0[...] = jnp.zeros(w0.shape, bf16)
    w1[...] = jnp.zeros(w1.shape, bf16)
    w2[...] = jnp.zeros(w2.shape, bf16)
    for q in range(4):
        for b in range(3):
            at = (q * 3 + b) * LANES
            for p in range(2):
                a = q - p
                if 0 <= a < 3:
                    rows = slice(p * LANES, p * LANES + ch)
                    w0[0, rows, at:at + ch] = w_ref[0, 3 * a + b]
                    w0[1, rows, at:at + ch] = w_ref[0, 3 * b + a]
                    w1[rows, at:at + ch] = w_ref[1, 3 * a + b]
                    w1[rows, 12 * LANES + at:12 * LANES + at + ch] = w_ref[1, 3 * b + a]
                    w2[p * ch:(p + 1) * ch, at:at + ch] = w_ref[2, 3 * a + b]
    eye = (lax.broadcasted_iota(jnp.int32, (ch, LANES), 0)
           == lax.broadcasted_iota(jnp.int32, (ch, LANES), 1))
    unit = jnp.where(eye, 1.0, 0.0)
    for p in range(2):
        at = (12 + p) * LANES
        w2[p * ch:(p + 1) * ch, at:at + LANES] = unit.astype(bf16)
    bias0 = bias_ref[0:1, :]
    bias1 = bias_ref[1:2, :]
    bias2 = jnp.broadcast_to(
        jnp.sum(unit * bias_ref[2:3, :], axis=1, keepdims=True), (ch, LANES))

    for m, (utab_f, vtab_f) in enumerate(((rows_f, cols_f), (cols_f, rows_f))):
        for b in range(3):
            vtab[m, b] = vtab_f[pl.ds(j0 + PAD - 9 + b, wide), :].astype(bf16)
        for i in range(tr + 14):
            row = utab_f[pl.ds(i0 + PAD - 7 + i, 1), :]
            utab[m, i] = jnp.broadcast_to(row, (16, LANES)).astype(bf16)

    def outer(m, i, b):
        v = vtab[m, b].reshape(wide // 16, 16, LANES)
        return (v * utab[m, i][None]).reshape(wide, LANES)

    pairs0 = (tr + 12) // 2
    step0 = pick(pairs0, 7)
    for m in range(2):
        def first(c, _, m=m):
            base = c * step0
            lhs = jnp.concatenate([
                jnp.concatenate([
                    jnp.maximum(outer(m, 2 * (base + g) + q, b), 0)
                    for q in range(4) for b in range(3)], axis=1)
                for g in range(step0)], axis=0)
            y = lax.dot_general(lhs, w0[m], NT, preferred_element_type=f32)
            for g in range(step0):
                for p in range(2):
                    i = 2 * (base + g) + p
                    own = outer(m, i + 1, 1).astype(f32)
                    part = y[g * wide:(g + 1) * wide, p * LANES:(p + 1) * LANES]
                    h1[m, pl.ds(PAD + i * wide, wide), :] = part + own + bias0
            return 0
        lax.fori_loop(0, pairs0 // step0, first, 0)

    def clear_edges(ref, count, width, edge, off, side):
        z = jnp.zeros((edge * width, LANES), f32)
        zc = jnp.zeros((side, LANES), f32)

        @pl.when(i0 == 0)
        def _():
            ref[pl.ds(off, edge * width), :] = z

        @pl.when(i0 + tr == bins)
        def _():
            ref[pl.ds(off + (count - edge) * width, edge * width), :] = z

        @pl.when(j0 == 0)
        def _():
            for i in range(count):
                ref[pl.ds(off + i * width, side), :] = zc

        @pl.when(j0 + tc == bins)
        def _():
            for i in range(count):
                ref[pl.ds(off + (i + 1) * width - side, side), :] = zc

    for m in range(2):
        clear_edges(h1.at[m], tr + 12, wide, 6, PAD, 8)

    groups1 = (tr + 8) // 4
    step1 = pick(groups1, 3)

    def second(c, _):
        base = c * step1
        rows = [4 * (base + g) + e for g in range(step1) for e in range(2)]
        lhs = []
        for m in range(2):
            for q in range(4):
                for b in range(3):
                    cut = jnp.concatenate([
                        h1[m, pl.ds(PAD + (r + 2 * q) * wide + 4 + 2 * (b - 1), span), :]
                        for r in rows], axis=0)
                    lhs.append(jnp.maximum(cut, 0.0).astype(bf16))
        y = lax.dot_general(jnp.concatenate(lhs, axis=1), w1[...], NT,
                            preferred_element_type=f32)
        for k, r in enumerate(rows):
            for p in range(2):
                at = PAD + (r + 2 + 2 * p) * wide + 4
                both = h1[0, pl.ds(at, span), :] + h1[1, pl.ds(at, span), :]
                part = y[k * span:(k + 1) * span, p * LANES:(p + 1) * LANES]
                sym[pl.ds((r + 2 * p) * span, span), :] = (part + both) * 0.5 + bias1
        return 0

    lax.fori_loop(0, groups1 // step1, second, 0)
    clear_edges(sym, tr + 8, span, 4, 0, 4)

    groups2 = tr // 8
    for_rows = 2 if groups2 % 2 == 0 else 1

    def third(c, _):
        rows = [8 * (c * for_rows + g) + e for g in range(for_rows) for e in range(4)]
        cells = []
        for r in rows:
            line = []
            for q in range(4):
                for b in range(3):
                    cut = sym[pl.ds((r + 4 * q) * span + 4 * b, tc), :]
                    line.append(jnp.maximum(cut, 0.0).astype(bf16))
            for p in range(2):
                line.append(sym[pl.ds((r + 4 + 4 * p) * span + 4, tc), :].astype(bf16))
            cells.append(jnp.concatenate(line, axis=1))
        y = lax.dot_general(w2[...], jnp.concatenate(cells, axis=0), NT,
                            preferred_element_type=f32)
        for k, r in enumerate(rows):
            for p in range(2):
                part = y[p * ch:(p + 1) * ch, k * tc:(k + 1) * tc]
                acc[pl.ds(r + 4 * p, ch, stride=tr), :] = part + bias2
        return 0

    lax.fori_loop(0, groups2 // for_rows, third, 0)
    out_ref[...] = acc[...].reshape(ch, tr, tc).astype(out_ref.dtype)


def decode(terms, w, bias, tr, tc):
    bins = terms.shape[0]
    ch = w.shape[2]
    f32, bf16 = jnp.float32, jnp.bfloat16
    vm = pl.BlockSpec(memory_space=pltpu.VMEM)
    return pl.pallas_call(
        functools.partial(decoder_kernel, tr, tc),
        out_shape=jax.ShapeDtypeStruct((ch, tr, tc), bf16),
        in_specs=[vm, vm, vm],
        out_specs=vm,
        scratch_shapes=[
            pltpu.VMEM((bins + 2 * PAD, LANES), f32),
            pltpu.VMEM((bins + 2 * PAD, LANES), f32),
            pltpu.VMEM((2, 3, tc + 16, LANES), bf16),
            pltpu.VMEM((2, tr + 14, 16, LANES), bf16),
            pltpu.VMEM((2, 2 * LANES, 12 * LANES), bf16),
            pltpu.VMEM((2 * LANES, 24 * LANES), bf16),
            pltpu.VMEM((2 * ch, 14 * LANES), bf16),
            pltpu.VMEM((2, (tr + 12) * (tc + 16) + 2 * PAD, LANES), f32),
            pltpu.VMEM(((tr + 8) * (tc + 8), LANES), f32),
            pltpu.VMEM((ch * tr, LANES), f32),
        ],
    )(terms, w, bias)


def project_kernel(bins_ref, row_ref, col_ref, send_ref):
    ch = row_ref.shape[0]
    halves = []
    for w_ref in (row_ref, col_ref):
        part = lax.dot_general(bins_ref[...], w_ref[...], NT,
                               preferred_element_type=jnp.float32)
        blank = jnp.zeros((part.shape[0], LANES - ch), jnp.float32)
        halves.append(jnp.concatenate([part, blank], axis=1))
    both = jnp.concatenate(halves, axis=1).astype(send_ref.dtype)
    for k in range(send_ref.shape[0]):
        send_ref[k] = both


def project(bins, row_proj, col_proj, peers):
    vm = pl.BlockSpec(memory_space=pltpu.VMEM)
    return pl.pallas_call(
        project_kernel,
        out_shape=jax.ShapeDtypeStruct((peers, bins.shape[0], 2 * LANES), jnp.bfloat16),
        in_specs=[vm, vm, vm],
        out_specs=vm,
    )(bins, row_proj, col_proj)


def shards(bins, row_proj, col_proj, conv_weight, conv_bias):
    rows = lax.axis_size("row")
    cols = lax.axis_size("col")
    reps = lax.axis_size("rep")
    part = conv_bias.shape[1]
    if reps > 1:
        row_proj = lax.all_gather(row_proj, "rep", axis=0, tiled=True)
        col_proj = lax.all_gather(col_proj, "rep", axis=0, tiled=True)
        conv_weight = lax.all_gather(conv_weight, "rep", axis=2, tiled=True)
        conv_bias = lax.all_gather(conv_bias, "rep", axis=1, tiled=True)
    peers = rows * cols
    total = bins.shape[0] * peers
    send = project(bins, row_proj, col_proj, peers)
    terms = lax.all_to_all(send, ("row", "col"), 0, 0, tiled=True)
    terms = terms.reshape(total, 2 * LANES)
    bias = jnp.pad(conv_bias, ((0, 0), (0, LANES - conv_bias.shape[1])))
    out = decode(terms, conv_weight, bias, total // rows, total // cols)
    if reps > 1:
        out = lax.dynamic_slice_in_dim(out, lax.axis_index("rep") * part, part, 0)
    return out


def solution(mesh):
    placed = (
        P(("groups", "row", "col"), None),
        P("rep", None),
        P("rep", None),
        P(None, None, "rep", None),
        P(None, "rep"),
    )
    return jax.shard_map(
        shards,
        mesh=mesh,
        in_specs=placed,
        out_specs=P("rep", ("groups", "row"), "col"),
        check_vma=False,
    )
```

```python
import functools
import jax
import jax.numpy as jnp
from jax import lax
from jax.experimental import pallas as pl
from jax.experimental.pallas import tpu as pltpu
from jax.sharding import PartitionSpec as P

LANES = 128
FRONT_BYTES = 48 << 20
DECODE_BYTES = 40 << 20
PAD = 16
WIDTH = 12 * LANES
DIRECT0 = 0
MIRROR0 = WIDTH
BOTH1 = 2 * WIDTH
PACKED = 4 * WIDTH
LAST = WIDTH + 2 * LANES
NT = (((1,), (1,)), ((), ()))


def pick(count, most):
    return max(k for k in range(1, min(count, most) + 1) if count % k == 0)


def filters_kernel(w_ref, b_ref, packed, taps_ref, bias_ref, column_ref):
    ch = w_ref.shape[2]
    f32, bf16 = jnp.float32, jnp.bfloat16
    packed[...] = jnp.zeros(packed.shape, bf16)
    for q in range(4):
        for b in range(3):
            at = (q * 3 + b) * LANES
            for p in range(2):
                a = q - p
                if 0 <= a < 3:
                    rows = slice(p * LANES, p * LANES + ch)
                    for first, layer, tap in (
                        (DIRECT0, 0, 3 * a + b),
                        (MIRROR0, 0, 3 * b + a),
                        (BOTH1, 1, 3 * a + b),
                        (BOTH1 + WIDTH, 1, 3 * b + a),
                    ):
                        packed[rows, first + at:first + at + ch] = w_ref[layer, tap]
    taps_ref[...] = jnp.zeros(taps_ref.shape, bf16)
    for tap in range(9):
        taps_ref[:, tap * LANES:tap * LANES + ch] = w_ref[2, tap]
    eye = (lax.broadcasted_iota(jnp.int32, (ch, LANES), 0)
           == lax.broadcasted_iota(jnp.int32, (ch, LANES), 1))
    unit = jnp.where(eye, 1.0, 0.0)
    blank = jnp.zeros((b_ref.shape[0], LANES - ch), f32)
    bias = jnp.concatenate([b_ref[...], blank], axis=1)
    bias_ref[...] = bias
    column_ref[...] = jnp.broadcast_to(
        jnp.sum(unit * bias[2:3, :], axis=1, keepdims=True), (ch, LANES))


def decoder_kernel(tr, tc, terms_ref, packed, taps_ref, bias_ref, column_ref, out_ref,
                   rows_f, cols_f, vtab, utab, h1, sym, acc, last):
    bins = terms_ref.shape[0]
    wide = tc + 16
    span = tc + 8
    i0 = lax.axis_index("row") * tr
    j0 = lax.axis_index("col") * tc
    f32, bf16 = jnp.float32, jnp.bfloat16

    for tab, lo in ((rows_f, 0), (cols_f, LANES)):
        tab[0:PAD] = jnp.zeros((PAD, LANES), f32)
        tab[PAD + bins:] = jnp.zeros((PAD, LANES), f32)
        tab[PAD:PAD + bins] = terms_ref[:, lo:lo + LANES].astype(f32)

    bias0 = bias_ref[0:1, :]
    bias1 = bias_ref[1:2, :]
    ch = out_ref.shape[0]
    bias2 = column_ref[...]

    for m, (utab_f, vtab_f) in enumerate(((rows_f, cols_f), (cols_f, rows_f))):
        for b in range(3):
            vtab[m, b] = vtab_f[pl.ds(j0 + PAD - 9 + b, wide), :].astype(bf16)
        for i in range(tr + 14):
            row = utab_f[pl.ds(i0 + PAD - 7 + i, 1), :]
            utab[m, i] = jnp.broadcast_to(row, (16, LANES)).astype(bf16)

    def outer(m, i, b):
        v = vtab[m, b].reshape(wide // 16, 16, LANES)
        return (v * utab[m, i][None]).reshape(wide, LANES)

    pairs0 = (tr + 12) // 2
    step0 = pick(pairs0, 7)
    for m in range(2):
        def first(c, _, m=m):
            base = c * step0
            lhs = jnp.concatenate([
                jnp.concatenate([
                    jnp.maximum(outer(m, 2 * (base + g) + q, b), 0)
                    for q in range(4) for b in range(3)], axis=1)
                for g in range(step0)], axis=0)
            y = lax.dot_general(lhs, packed[:, m * WIDTH:(m + 1) * WIDTH], NT, preferred_element_type=f32)
            for g in range(step0):
                for p in range(2):
                    i = 2 * (base + g) + p
                    own = outer(m, i + 1, 1).astype(f32)
                    part = y[g * wide:(g + 1) * wide, p * LANES:(p + 1) * LANES]
                    h1[m, pl.ds(PAD + i * wide, wide), :] = part + own + bias0
            return 0
        lax.fori_loop(0, pairs0 // step0, first, 0)

    def clear_edges(ref, count, width, edge, off, side):
        z = jnp.zeros((edge * width, LANES), f32)
        zc = jnp.zeros((side, LANES), f32)

        @pl.when(i0 == 0)
        def _():
            ref[pl.ds(off, edge * width), :] = z

        @pl.when(i0 + tr == bins)
        def _():
            ref[pl.ds(off + (count - edge) * width, edge * width), :] = z

        @pl.when(j0 == 0)
        def _():
            for i in range(count):
                ref[pl.ds(off + i * width, side), :] = zc

        @pl.when(j0 + tc == bins)
        def _():
            for i in range(count):
                ref[pl.ds(off + (i + 1) * width - side, side), :] = zc

    for m in range(2):
        clear_edges(h1.at[m], tr + 12, wide, 6, PAD, 8)

    groups1 = (tr + 8) // 4
    step1 = pick(groups1, 3)

    def second(c, _):
        base = c * step1
        rows = [4 * (base + g) + e for g in range(step1) for e in range(2)]
        lhs = []
        for m in range(2):
            for q in range(4):
                for b in range(3):
                    cut = jnp.concatenate([
                        h1[m, pl.ds(PAD + (r + 2 * q) * wide + 4 + 2 * (b - 1), span), :]
                        for r in rows], axis=0)
                    lhs.append(jnp.maximum(cut, 0.0).astype(bf16))
        y = lax.dot_general(jnp.concatenate(lhs, axis=1), packed[:, BOTH1:PACKED], NT,
                            preferred_element_type=f32)
        for k, r in enumerate(rows):
            for p in range(2):
                at = PAD + (r + 2 + 2 * p) * wide + 4
                both = h1[0, pl.ds(at, span), :] + h1[1, pl.ds(at, span), :]
                part = y[k * span:(k + 1) * span, p * LANES:(p + 1) * LANES]
                sym[pl.ds((r + 2 * p) * span, span), :] = (part + both) * 0.5 + bias1
        return 0

    lax.fori_loop(0, groups1 // step1, second, 0)
    clear_edges(sym, tr + 8, span, 4, 0, 4)

    last[...] = jnp.zeros(last.shape, bf16)
    eye = (lax.broadcasted_iota(jnp.int32, (ch, LANES), 0)
           == lax.broadcasted_iota(jnp.int32, (ch, LANES), 1))
    for p in range(2):
        rows = slice(p * ch, (p + 1) * ch)
        at = 3 * p * LANES
        last[rows, at:at + 9 * LANES] = taps_ref[...]
        at = WIDTH + p * LANES
        last[rows, at:at + LANES] = jnp.where(eye, 1.0, 0.0).astype(bf16)
    groups2 = tr // 8
    for_rows = 2 if groups2 % 2 == 0 else 1

    def third(c, _):
        rows = [8 * (c * for_rows + g) + e for g in range(for_rows) for e in range(4)]
        cells = []
        for r in rows:
            line = []
            for q in range(4):
                for b in range(3):
                    cut = sym[pl.ds((r + 4 * q) * span + 4 * b, tc), :]
                    line.append(jnp.maximum(cut, 0.0).astype(bf16))
            for p in range(2):
                line.append(sym[pl.ds((r + 4 + 4 * p) * span + 4, tc), :].astype(bf16))
            cells.append(jnp.concatenate(line, axis=1))
        y = lax.dot_general(last[...], jnp.concatenate(cells, axis=0), NT,
                            preferred_element_type=f32)
        for k, r in enumerate(rows):
            for p in range(2):
                part = y[p * ch:(p + 1) * ch, k * tc:(k + 1) * tc]
                acc[pl.ds(r + 4 * p, ch, stride=tr), :] = part + bias2
        return 0

    lax.fori_loop(0, groups2 // for_rows, third, 0)
    out_ref[...] = acc[...].reshape(ch, tr, tc).astype(out_ref.dtype)


def filters(w, bias):
    ch = w.shape[2]
    f32, bf16 = jnp.float32, jnp.bfloat16
    vm = pl.BlockSpec(memory_space=pltpu.VMEM)
    shapes = (
        ((2 * LANES, PACKED), bf16),
        ((ch, 9 * LANES), bf16),
        ((bias.shape[0], LANES), f32),
        ((ch, LANES), f32),
    )
    return pl.pallas_call(
        filters_kernel,
        out_shape=[jax.ShapeDtypeStruct(*s) for s in shapes],
        in_specs=[vm, vm],
        out_specs=[vm] * len(shapes),
        compiler_params=pltpu.CompilerParams(vmem_limit_bytes=FRONT_BYTES),
        cost_estimate=pl.CostEstimate(flops=0, bytes_accessed=8 << 20, transcendentals=0),
    )(w, bias)


def decode(terms, packed, tr, tc):
    bins = terms.shape[0]
    ch = packed[1].shape[0]
    f32, bf16 = jnp.float32, jnp.bfloat16
    vm = pl.BlockSpec(memory_space=pltpu.VMEM)
    scratch = (
        ((bins + 2 * PAD, LANES), f32),
        ((bins + 2 * PAD, LANES), f32),
        ((2, 3, tc + 16, LANES), bf16),
        ((2, tr + 14, 16, LANES), bf16),
        ((2, (tr + 12) * (tc + 16) + 2 * PAD, LANES), f32),
        (((tr + 8) * (tc + 8), LANES), f32),
        ((ch * tr, LANES), f32),
        ((2 * ch, LAST), bf16),
    )
    return pl.pallas_call(
        functools.partial(decoder_kernel, tr, tc),
        out_shape=jax.ShapeDtypeStruct((ch, tr, tc), bf16),
        in_specs=[vm] * 5,
        out_specs=vm,
        scratch_shapes=[pltpu.VMEM(*s) for s in scratch],
        compiler_params=pltpu.CompilerParams(vmem_limit_bytes=DECODE_BYTES),
    )(terms, *packed)


def project_kernel(bins_hbm, row_hbm, col_hbm, send_ref, bins, w, sems):
    ch = row_hbm.shape[0]
    copies = [
        pltpu.make_async_copy(row_hbm, w.at[0:ch], sems.at[0]),
        pltpu.make_async_copy(col_hbm, w.at[LANES:LANES + ch], sems.at[1]),
        pltpu.make_async_copy(bins_hbm, bins, sems.at[2]),
    ]
    for copy in copies:
        copy.start()
    for p in range(2):
        w[p * LANES + ch:(p + 1) * LANES] = jnp.zeros((LANES - ch, w.shape[1]), w.dtype)
    for copy in copies:
        copy.wait()
    both = lax.dot_general(bins[...], w[...], NT, preferred_element_type=jnp.float32)
    both = both.astype(send_ref.dtype)
    for k in range(send_ref.shape[0]):
        send_ref[k] = both


def project(bins, row_proj, col_proj, peers):
    return pl.pallas_call(
        project_kernel,
        out_shape=jax.ShapeDtypeStruct((peers, bins.shape[0], 2 * LANES), jnp.bfloat16),
        in_specs=[pl.BlockSpec(memory_space=pltpu.HBM)] * 3,
        out_specs=pl.BlockSpec(memory_space=pltpu.VMEM),
        scratch_shapes=[
            pltpu.VMEM(bins.shape, bins.dtype),
            pltpu.VMEM((2 * LANES, bins.shape[1]), bins.dtype),
            pltpu.SemaphoreType.DMA((3,)),
        ],
    )(bins, row_proj, col_proj)


def shards(bins, row_proj, col_proj, conv_weight, conv_bias):
    rows = lax.axis_size("row")
    cols = lax.axis_size("col")
    reps = lax.axis_size("rep")
    part = conv_bias.shape[1]
    if reps > 1:
        row_proj = lax.all_gather(row_proj, "rep", axis=0, tiled=True)
        col_proj = lax.all_gather(col_proj, "rep", axis=0, tiled=True)
        conv_weight = lax.all_gather(conv_weight, "rep", axis=2, tiled=True)
        conv_bias = lax.all_gather(conv_bias, "rep", axis=1, tiled=True)
    peers = rows * cols
    total = bins.shape[0] * peers
    send = project(bins, row_proj, col_proj, peers)
    terms = lax.all_to_all(send, ("row", "col"), 0, 0, tiled=True)
    terms = terms.reshape(total, 2 * LANES)
    packed = filters(conv_weight, conv_bias)
    out = decode(terms, packed, total // rows, total // cols)
    if reps > 1:
        out = lax.dynamic_slice_in_dim(out, lax.axis_index("rep") * part, part, 0)
    return out


def solution(mesh):
    placed = (
        P(("groups", "row", "col"), None),
        P("rep", None),
        P("rep", None),
        P(None, None, "rep", None),
        P(None, "rep"),
    )
    return jax.shard_map(
        shards,
        mesh=mesh,
        in_specs=placed,
        out_specs=P("rep", ("groups", "row"), "col"),
        check_vma=False,
    )
```

```python
import functools
import jax
import jax.numpy as jnp
from jax import lax
from jax.experimental import pallas as pl
from jax.experimental.pallas import tpu as pltpu
from jax.sharding import PartitionSpec as P

LANES = 128
PAD = 16
BLOCKS = 9
STEP0 = 4
STEP1 = 1
STEP2 = 1
APART = True
WIDTH = BLOCKS * LANES
FRONT_BYTES = 48 << 20
DECODE_BYTES = 40 << 20
NT = (((1,), (1,)), ((), ()))


def cuts(count, most):
    parts = -(-count // most)
    edges = [count * k // parts for k in range(parts + 1)]
    return list(zip(edges[:-1], edges[1:]))


def lane_ids(shape):
    return lax.broadcasted_iota(jnp.int32, shape, len(shape) - 1)


def third_of(value, ch, t):
    spare = LANES - ch
    return pltpu.roll(value, (ch - t * spare) % LANES, value.ndim - 1)


def filters_kernel(w_ref, b_ref, packed0, packed1, last, bias_ref, column_ref, wide):
    ch = w_ref.shape[2]
    spare = LANES - ch
    f32, bf16 = jnp.float32, jnp.bfloat16
    wide[...] = jnp.zeros(wide.shape, f32)

    def fill(ref, rows0, rows1, first, layer, swap):
        for b in range(3):
            taps = []
            for a in range(3):
                wide[:, 0:ch] = w_ref[layer, 3 * b + a if swap else 3 * a + b].astype(f32)
                taps.append(wide[...])
            for t in range(3):
                cols = slice(first + (3 * t + b) * LANES, first + (3 * t + b + 1) * LANES)
                ref[rows0, cols] = taps[t].astype(bf16)
                main = taps[t - 1] if t else jnp.zeros((ch, LANES), f32)
                moved = third_of(taps[2], ch, t)
                ref[rows1, cols] = jnp.where(lane_ids((ch, LANES)) < ch, main, moved).astype(bf16)

    low, high = slice(0, ch), slice(LANES, LANES + ch)
    for ref in (packed0, packed1):
        for p in range(2):
            ref[p * LANES + ch:(p + 1) * LANES] = jnp.zeros((spare, ref.shape[1]), bf16)
    fill(packed0, low, high, 0, 0, False)
    fill(packed0, low, high, WIDTH, 0, True)
    fill(packed1, low, high, 0, 1, False)
    fill(packed1, low, high, WIDTH, 1, True)
    fill(last, slice(0, ch), slice(ch, 2 * ch), 0, 2, False)
    eye = lax.broadcasted_iota(jnp.int32, (ch, LANES), 0) == lane_ids((ch, LANES))
    unit = jnp.where(eye, 1.0, 0.0)
    for p in range(2):
        for s in range(2):
            part = unit if p == s else jnp.zeros((ch, LANES), f32)
            last[p * ch:(p + 1) * ch, WIDTH + s * LANES:WIDTH + (s + 1) * LANES] = part.astype(bf16)
    blank = jnp.zeros((b_ref.shape[0], spare), f32)
    bias = jnp.concatenate([b_ref[...], blank], axis=1)
    bias_ref[...] = bias
    column_ref[...] = jnp.broadcast_to(
        jnp.sum(unit * bias[2:3, :], axis=1, keepdims=True), (ch, LANES))


def decoder_kernel(tr, tc, terms_ref, packed0, packed1, last, bias_ref, column_ref, out_ref,
                   rows_f, cols_f, mixed_v, mixed_u, plain_v, plain_u, h1, sym, acc):
    bins = terms_ref.shape[0]
    ch = out_ref.shape[0]
    wide = tc + 16
    span = tc + 8
    f32, bf16 = jnp.float32, jnp.bfloat16
    i0 = lax.axis_index("row") * tr
    j0 = lax.axis_index("col") * tc
    top, bottom = i0 == 0, i0 + tr == bins
    left, right = j0 == 0, j0 + tc == bins
    bias0 = bias_ref[0:1, :]
    bias1 = bias_ref[1:2, :]

    def stage(body):
        if APART:
            pl.when(i0 >= 0)(body)
        else:
            body()

    for tab, lo in ((rows_f, 0), (cols_f, LANES)):
        tab[0:PAD] = jnp.zeros((PAD, LANES), f32)
        tab[PAD + bins:] = jnp.zeros((PAD, LANES), f32)
        tab[PAD:PAD + bins] = terms_ref[:, lo:lo + LANES].astype(f32)

    pairs0 = (tr + 12) // 2
    tall = mixed_u.shape[2]
    body_v = lane_ids((wide + 8, LANES)) < ch
    body_u = lane_ids((tall, LANES)) < ch
    for m, (u_src, v_src) in enumerate(((rows_f, cols_f), (cols_f, rows_f))):
        line = v_src[pl.ds(j0 + PAD - 9, wide + 8), :]
        plain_v[m] = line
        for t in range(3):
            mixed_v[m, t] = jnp.where(body_v, line, third_of(line, ch, t))
        fourth = u_src[pl.ds(i0 + PAD - 7 + 3, tall), :]
        for t in range(3):
            row = u_src[pl.ds(i0 + PAD - 7 + t, tall), :]
            mixed_u[m, t] = jnp.where(body_u, row, third_of(fourth, ch, t))
        plain_u[m] = u_src[pl.ds(i0 + PAD - 6, tall), :]

    def put(ref, where, k, value, width):
        at = k // 2 + 1
        cells = slice(0, width)
        if k % 2 == 0:
            ref[where + (at, 0, cells, slice(0, ch))] = value[:, 0:ch]
            ref[where + (at - 1, 2, cells, slice(0, ch))] = value[:, 0:ch]
        else:
            ref[where + (at, 1, cells, slice(0, ch))] = value[:, 0:ch]
            for t in range(3):
                ref[where + (at - 1, t, cells, slice(ch, LANES))] = third_of(value, ch, t)[:, ch:LANES]

    def clear(ref, heads, groups, width, side, deep):
        main, rest = slice(0, ch), slice(ch, LANES)
        body = jnp.zeros((width, ch), f32)
        tail = jnp.zeros((width, LANES - ch), f32)
        edge = jnp.zeros((side, LANES), f32)
        above = [(1, 0, main)] + ([(1, 1, main), (2, 0, main), (1, 2, main)] if deep == 3 else [])
        below = [(groups, t, rest) for t in range(3)]
        if deep == 3:
            below += [(groups, 1, main), (groups, 2, main)] + [(groups - 1, t, rest) for t in range(3)]
        for flag, places in ((top, above), (bottom, below)):
            @pl.when(flag)
            def _(places=places):
                for head in heads:
                    for at, t, lanes in places:
                        ref[head + (at, t, slice(0, width), lanes)] = body if lanes == main else tail
        for flag, start in ((left, 0), (right, width - side)):
            @pl.when(flag)
            def _(start=start):
                for head in heads:
                    for at in range(1, groups + 1):
                        for t in range(3):
                            ref[head + (at, t, slice(start, start + side), slice(0, LANES))] = edge

    def first(m, lo, hi):
        rows = []
        for n in range(lo, hi):
            line = []
            for t in range(3):
                u = jnp.broadcast_to(mixed_u[m, t, 2 * n:2 * n + 1, :], (wide, LANES)).astype(bf16)
                for b in range(3):
                    v = mixed_v[m, t, b:b + wide, :].astype(bf16)
                    line.append(jnp.maximum(v * u, 0))
            rows.append(jnp.concatenate(line, axis=1))
        y = lax.dot_general(jnp.concatenate(rows, axis=0), packed0[:, m * WIDTH:(m + 1) * WIDTH], NT,
                            preferred_element_type=f32)
        for k, n in enumerate(range(lo, hi)):
            for e in range(2):
                own = plain_v[m, 1:1 + wide, :] * plain_u[m, 2 * n + e:2 * n + e + 1, :]
                part = y[k * wide:(k + 1) * wide, e * LANES:(e + 1) * LANES]
                put(h1, (m, e), n, part + own + bias0, wide)

    for m in range(2):
        for lo, hi in cuts(pairs0, STEP0):
            stage(functools.partial(first, m, lo, hi))
    groups1 = (tr + 8) // 4
    clear(h1, [(m, e) for m in range(2) for e in range(2)], groups1, wide, 8, 3)

    def second(lo, hi):
        spots = [(k, e) for k in range(lo, hi) for e in range(2)]
        lhs = []
        for m in range(2):
            for t in range(3):
                for b in range(3):
                    cut = jnp.concatenate([
                        h1[m, e, k + 1, t, 2 + 2 * b:2 + 2 * b + span, :] for k, e in spots], axis=0)
                    lhs.append(jnp.maximum(cut.astype(bf16), 0))
        y = lax.dot_general(jnp.concatenate(lhs, axis=1), packed1[...], NT, preferred_element_type=f32)
        for s, (k, e) in enumerate(spots):
            for p in range(2):
                both = h1[0, e, k + 1, 1 + p, 4:4 + span, :] + h1[1, e, k + 1, 1 + p, 4:4 + span, :]
                part = y[s * span:(s + 1) * span, p * LANES:(p + 1) * LANES]
                put(sym, (e + 2 * p,), k, (part + both) * 0.5 + bias1, span)

    for lo, hi in cuts(groups1, STEP1):
        stage(functools.partial(second, lo, hi))
    groups2 = tr // 8
    clear(sym, [(e,) for e in range(4)], groups2, span, 4, 1)

    bias2 = column_ref[...]
    def third(lo, hi):
        spots = [(g, e) for g in range(lo, hi) for e in range(4)]
        cells = []
        for g, e in spots:
            line = []
            for t in range(3):
                for b in range(3):
                    line.append(jnp.maximum(sym[e, g + 1, t, 4 * b:4 * b + tc, :].astype(bf16), 0))
            for p in range(2):
                line.append(sym[e, g + 1, 1 + p, 4:4 + tc, :].astype(bf16))
            cells.append(jnp.concatenate(line, axis=1))
        y = lax.dot_general(last[...], jnp.concatenate(cells, axis=0), NT, preferred_element_type=f32)
        for s, (g, e) in enumerate(spots):
            for p in range(2):
                part = y[p * ch:(p + 1) * ch, s * tc:(s + 1) * tc]
                acc[pl.ds(8 * g + e + 4 * p, ch, stride=tr), :] = part + bias2

    for lo, hi in cuts(groups2, STEP2):
        stage(functools.partial(third, lo, hi))
    out_ref[...] = acc[...].reshape(ch, tr, tc).astype(out_ref.dtype)


def filters(w, bias):
    ch = w.shape[2]
    f32, bf16 = jnp.float32, jnp.bfloat16
    vm = pl.BlockSpec(memory_space=pltpu.VMEM)
    shapes = (
        ((2 * LANES, 2 * WIDTH), bf16),
        ((2 * LANES, 2 * WIDTH), bf16),
        ((2 * ch, WIDTH + 2 * LANES), bf16),
        ((bias.shape[0], LANES), f32),
        ((ch, LANES), f32),
    )
    return pl.pallas_call(
        filters_kernel,
        out_shape=[jax.ShapeDtypeStruct(*s) for s in shapes],
        in_specs=[vm, vm],
        out_specs=[vm] * len(shapes),
        scratch_shapes=[pltpu.VMEM((ch, LANES), f32)],
        compiler_params=pltpu.CompilerParams(vmem_limit_bytes=FRONT_BYTES),
        cost_estimate=pl.CostEstimate(flops=0, bytes_accessed=8 << 20, transcendentals=0),
    )(w, bias)


def decode(terms, packed, tr, tc):
    bins = terms.shape[0]
    ch = packed[4].shape[0]
    f32, bf16 = jnp.float32, jnp.bfloat16
    vm = pl.BlockSpec(memory_space=pltpu.VMEM)
    wide, span = tc + 16, tc + 8
    pairs0, groups1 = (tr + 12) // 2, (tr + 8) // 4
    tall = -(-(tr + 12) // 8) * 8
    scratch = (
        ((bins + 2 * PAD, LANES), f32),
        ((bins + 2 * PAD, LANES), f32),
        ((2, 3, wide + 8, LANES), f32),
        ((2, 3, tall, LANES), f32),
        ((2, wide + 8, LANES), f32),
        ((2, tall, LANES), f32),
        ((2, 2, pairs0 // 2 + 1, 3, wide, LANES), f32),
        ((4, groups1 // 2 + 1, 3, span, LANES), f32),
        ((ch * tr, LANES), f32),
    )
    return pl.pallas_call(
        functools.partial(decoder_kernel, tr, tc),
        out_shape=jax.ShapeDtypeStruct((ch, tr, tc), bf16),
        in_specs=[vm] * 6,
        out_specs=vm,
        scratch_shapes=[pltpu.VMEM(*s) for s in scratch],
        compiler_params=pltpu.CompilerParams(vmem_limit_bytes=DECODE_BYTES),
    )(terms, *packed)


def project_kernel(bins_hbm, row_hbm, col_hbm, send_ref, bins, w, sems):
    ch = row_hbm.shape[0]
    copies = [
        pltpu.make_async_copy(row_hbm, w.at[0:ch], sems.at[0]),
        pltpu.make_async_copy(col_hbm, w.at[LANES:LANES + ch], sems.at[1]),
        pltpu.make_async_copy(bins_hbm, bins, sems.at[2]),
    ]
    for copy in copies:
        copy.start()
    for p in range(2):
        w[p * LANES + ch:(p + 1) * LANES] = jnp.zeros((LANES - ch, w.shape[1]), w.dtype)
    for copy in copies:
        copy.wait()
    both = lax.dot_general(bins[...], w[...], NT, preferred_element_type=jnp.float32)
    both = both.astype(send_ref.dtype)
    for k in range(send_ref.shape[0]):
        send_ref[k] = both


def project(bins, row_proj, col_proj, peers):
    return pl.pallas_call(
        project_kernel,
        out_shape=jax.ShapeDtypeStruct((peers, bins.shape[0], 2 * LANES), jnp.bfloat16),
        in_specs=[pl.BlockSpec(memory_space=pltpu.HBM)] * 3,
        out_specs=pl.BlockSpec(memory_space=pltpu.VMEM),
        scratch_shapes=[
            pltpu.VMEM(bins.shape, bins.dtype),
            pltpu.VMEM((2 * LANES, bins.shape[1]), bins.dtype),
            pltpu.SemaphoreType.DMA((3,)),
        ],
    )(bins, row_proj, col_proj)


def shards(bins, row_proj, col_proj, conv_weight, conv_bias):
    rows = lax.axis_size("row")
    cols = lax.axis_size("col")
    reps = lax.axis_size("rep")
    part = conv_bias.shape[1]
    if reps > 1:
        row_proj = lax.all_gather(row_proj, "rep", axis=0, tiled=True)
        col_proj = lax.all_gather(col_proj, "rep", axis=0, tiled=True)
        conv_weight = lax.all_gather(conv_weight, "rep", axis=2, tiled=True)
        conv_bias = lax.all_gather(conv_bias, "rep", axis=1, tiled=True)
    peers = rows * cols
    total = bins.shape[0] * peers
    send = project(bins, row_proj, col_proj, peers)
    terms = lax.all_to_all(send, ("row", "col"), 0, 0, tiled=True)
    terms = terms.reshape(total, 2 * LANES)
    packed = filters(conv_weight, conv_bias)
    out = decode(terms, packed, total // rows, total // cols)
    if reps > 1:
        out = lax.dynamic_slice_in_dim(out, lax.axis_index("rep") * part, part, 0)
    return out


def solution(mesh):
    placed = (
        P(("groups", "row", "col"), None),
        P("rep", None),
        P("rep", None),
        P(None, None, "rep", None),
        P(None, "rep"),
    )
    return jax.shard_map(
        shards,
        mesh=mesh,
        in_specs=placed,
        out_specs=P("rep", ("groups", "row"), "col"),
        check_vma=False,
    )
```

```python
import functools
import jax
import jax.numpy as jnp
from jax import lax
from jax.experimental import pallas as pl
from jax.experimental.pallas import tpu as pltpu
from jax.sharding import PartitionSpec as P

LANES = 128
PAD = 16
BLOCKS = 9
STEP0 = 4
STEP1 = 1
STEP2 = 1
APART = True
WIDTH = BLOCKS * LANES
LAST = 4 * WIDTH
PACKED = LAST + WIDTH + 2 * LANES
FRONT_BYTES = 48 << 20
DECODE_BYTES = 40 << 20
NT = (((1,), (1,)), ((), ()))


def cuts(count, most):
    parts = -(-count // most)
    edges = [count * k // parts for k in range(parts + 1)]
    return list(zip(edges[:-1], edges[1:]))


def lane_ids(shape):
    return lax.broadcasted_iota(jnp.int32, shape, len(shape) - 1)


def third_of(value, ch, t):
    spare = LANES - ch
    return pltpu.roll(value, (ch - t * spare) % LANES, value.ndim - 1)


def filters_kernel(w_ref, b_ref, packed, bias_ref, column_ref, wide):
    ch = w_ref.shape[2]
    spare = LANES - ch
    f32, bf16 = jnp.float32, jnp.bfloat16
    wide[...] = jnp.zeros(wide.shape, f32)

    def fill(rows0, rows1, first, layer, swap):
        for b in range(3):
            taps = []
            for a in range(3):
                wide[:, 0:ch] = w_ref[layer, 3 * b + a if swap else 3 * a + b].astype(f32)
                taps.append(wide[...])
            for t in range(3):
                cols = slice(first + (3 * t + b) * LANES, first + (3 * t + b + 1) * LANES)
                packed[rows0, cols] = taps[t].astype(bf16)
                main = taps[t - 1] if t else jnp.zeros((ch, LANES), f32)
                moved = third_of(taps[2], ch, t)
                packed[rows1, cols] = jnp.where(lane_ids((ch, LANES)) < ch, main, moved).astype(bf16)

    low, high = slice(0, ch), slice(LANES, LANES + ch)
    for p in range(2):
        packed[p * LANES + ch:(p + 1) * LANES, 0:LAST] = jnp.zeros((spare, LAST), bf16)
    for layer in range(2):
        fill(low, high, 2 * layer * WIDTH, layer, False)
        fill(low, high, (2 * layer + 1) * WIDTH, layer, True)
    fill(slice(0, ch), slice(ch, 2 * ch), LAST, 2, False)
    eye = lax.broadcasted_iota(jnp.int32, (ch, LANES), 0) == lane_ids((ch, LANES))
    unit = jnp.where(eye, 1.0, 0.0)
    for p in range(2):
        for s in range(2):
            part = unit if p == s else jnp.zeros((ch, LANES), f32)
            packed[p * ch:(p + 1) * ch, PACKED - (2 - s) * LANES:PACKED - (1 - s) * LANES] = part.astype(bf16)
    blank = jnp.zeros((b_ref.shape[0], spare), f32)
    bias = jnp.concatenate([b_ref[...], blank], axis=1)
    bias_ref[...] = bias
    column_ref[...] = jnp.broadcast_to(
        jnp.sum(unit * bias[2:3, :], axis=1, keepdims=True), (ch, LANES))


def decoder_kernel(tr, tc, terms_ref, packed, bias_ref, column_ref, out_ref,
                   rows_f, cols_f, mixed_v, mixed_u, plain_v, plain_u, h1, sym, acc):
    bins = terms_ref.shape[0]
    ch = out_ref.shape[0]
    wide = tc + 16
    span = tc + 8
    f32, bf16 = jnp.float32, jnp.bfloat16
    i0 = lax.axis_index("row") * tr
    j0 = lax.axis_index("col") * tc
    top, bottom = i0 == 0, i0 + tr == bins
    left, right = j0 == 0, j0 + tc == bins
    bias0 = bias_ref[0:1, :]
    bias1 = bias_ref[1:2, :]

    def stage(body):
        if APART:
            pl.when(i0 >= 0)(body)
        else:
            body()

    for tab, lo in ((rows_f, 0), (cols_f, LANES)):
        tab[0:PAD] = jnp.zeros((PAD, LANES), f32)
        tab[PAD + bins:] = jnp.zeros((PAD, LANES), f32)
        tab[PAD:PAD + bins] = terms_ref[:, lo:lo + LANES].astype(f32)

    pairs0 = (tr + 12) // 2
    tall = mixed_u.shape[2]
    body_v = lane_ids((wide + 8, LANES)) < ch
    body_u = lane_ids((tall, LANES)) < ch
    for m, (u_src, v_src) in enumerate(((rows_f, cols_f), (cols_f, rows_f))):
        line = v_src[pl.ds(j0 + PAD - 9, wide + 8), :]
        plain_v[m] = line
        for t in range(3):
            mixed_v[m, t] = jnp.where(body_v, line, third_of(line, ch, t))
        fourth = u_src[pl.ds(i0 + PAD - 7 + 3, tall), :]
        for t in range(3):
            row = u_src[pl.ds(i0 + PAD - 7 + t, tall), :]
            mixed_u[m, t] = jnp.where(body_u, row, third_of(fourth, ch, t))
        plain_u[m] = u_src[pl.ds(i0 + PAD - 6, tall), :]

    def put(ref, where, k, value, width):
        at = k // 2 + 1
        cells = slice(0, width)
        if k % 2 == 0:
            ref[where + (at, 0, cells, slice(0, ch))] = value[:, 0:ch]
            ref[where + (at - 1, 2, cells, slice(0, ch))] = value[:, 0:ch]
        else:
            ref[where + (at, 1, cells, slice(0, ch))] = value[:, 0:ch]
            for t in range(3):
                ref[where + (at - 1, t, cells, slice(ch, LANES))] = third_of(value, ch, t)[:, ch:LANES]

    def clear(ref, heads, groups, width, side, deep):
        main, rest = slice(0, ch), slice(ch, LANES)
        body = jnp.zeros((width, ch), f32)
        tail = jnp.zeros((width, LANES - ch), f32)
        edge = jnp.zeros((side, LANES), f32)
        above = [(1, 0, main)] + ([(1, 1, main), (2, 0, main), (1, 2, main)] if deep == 3 else [])
        below = [(groups, t, rest) for t in range(3)]
        if deep == 3:
            below += [(groups, 1, main), (groups, 2, main)] + [(groups - 1, t, rest) for t in range(3)]
        for flag, places in ((top, above), (bottom, below)):
            @pl.when(flag)
            def _(places=places):
                for head in heads:
                    for at, t, lanes in places:
                        ref[head + (at, t, slice(0, width), lanes)] = body if lanes == main else tail
        for flag, start in ((left, 0), (right, width - side)):
            @pl.when(flag)
            def _(start=start):
                for head in heads:
                    for at in range(1, groups + 1):
                        for t in range(3):
                            ref[head + (at, t, slice(start, start + side), slice(0, LANES))] = edge

    def first(m, lo, hi):
        rows = []
        for n in range(lo, hi):
            line = []
            for t in range(3):
                u = jnp.broadcast_to(mixed_u[m, t, 2 * n:2 * n + 1, :], (wide, LANES)).astype(bf16)
                for b in range(3):
                    v = mixed_v[m, t, b:b + wide, :].astype(bf16)
                    line.append(jnp.maximum(v * u, 0))
            rows.append(jnp.concatenate(line, axis=1))
        y = lax.dot_general(jnp.concatenate(rows, axis=0), packed[:, m * WIDTH:(m + 1) * WIDTH], NT,
                            preferred_element_type=f32)
        for k, n in enumerate(range(lo, hi)):
            for e in range(2):
                own = plain_v[m, 1:1 + wide, :] * plain_u[m, 2 * n + e:2 * n + e + 1, :]
                part = y[k * wide:(k + 1) * wide, e * LANES:(e + 1) * LANES]
                put(h1, (m, e), n, part + own + bias0, wide)

    for m in range(2):
        for lo, hi in cuts(pairs0, STEP0):
            stage(functools.partial(first, m, lo, hi))
    groups1 = (tr + 8) // 4
    clear(h1, [(m, e) for m in range(2) for e in range(2)], groups1, wide, 8, 3)

    def second(lo, hi):
        spots = [(k, e) for k in range(lo, hi) for e in range(2)]
        lhs = []
        for m in range(2):
            for t in range(3):
                for b in range(3):
                    cut = jnp.concatenate([
                        h1[m, e, k + 1, t, 2 + 2 * b:2 + 2 * b + span, :] for k, e in spots], axis=0)
                    lhs.append(jnp.maximum(cut.astype(bf16), 0))
        y = lax.dot_general(jnp.concatenate(lhs, axis=1), packed[:, 2 * WIDTH:LAST], NT, preferred_element_type=f32)
        for s, (k, e) in enumerate(spots):
            for p in range(2):
                both = h1[0, e, k + 1, 1 + p, 4:4 + span, :] + h1[1, e, k + 1, 1 + p, 4:4 + span, :]
                part = y[s * span:(s + 1) * span, p * LANES:(p + 1) * LANES]
                put(sym, (e + 2 * p,), k, (part + both) * 0.5 + bias1, span)

    for lo, hi in cuts(groups1, STEP1):
        stage(functools.partial(second, lo, hi))
    groups2 = tr // 8
    clear(sym, [(e,) for e in range(4)], groups2, span, 4, 1)

    bias2 = column_ref[...]
    def third(lo, hi):
        spots = [(g, e) for g in range(lo, hi) for e in range(4)]
        cells = []
        for g, e in spots:
            line = []
            for t in range(3):
                for b in range(3):
                    line.append(jnp.maximum(sym[e, g + 1, t, 4 * b:4 * b + tc, :].astype(bf16), 0))
            for p in range(2):
                line.append(sym[e, g + 1, 1 + p, 4:4 + tc, :].astype(bf16))
            cells.append(jnp.concatenate(line, axis=1))
        y = lax.dot_general(packed[0:2 * ch, LAST:PACKED], jnp.concatenate(cells, axis=0), NT, preferred_element_type=f32)
        for s, (g, e) in enumerate(spots):
            for p in range(2):
                part = y[p * ch:(p + 1) * ch, s * tc:(s + 1) * tc]
                acc[pl.ds(8 * g + e + 4 * p, ch, stride=tr), :] = part + bias2

    for lo, hi in cuts(groups2, STEP2):
        stage(functools.partial(third, lo, hi))
    out_ref[...] = acc[...].reshape(ch, tr, tc).astype(out_ref.dtype)


def filters(w, bias):
    ch = w.shape[2]
    f32, bf16 = jnp.float32, jnp.bfloat16
    vm = pl.BlockSpec(memory_space=pltpu.VMEM)
    shapes = (
        ((2 * LANES, PACKED), bf16),
        ((bias.shape[0], LANES), f32),
        ((ch, LANES), f32),
    )
    return pl.pallas_call(
        filters_kernel,
        out_shape=[jax.ShapeDtypeStruct(*s) for s in shapes],
        in_specs=[vm, vm],
        out_specs=[vm] * len(shapes),
        scratch_shapes=[pltpu.VMEM((ch, LANES), f32)],
        compiler_params=pltpu.CompilerParams(vmem_limit_bytes=FRONT_BYTES),
        cost_estimate=pl.CostEstimate(flops=0, bytes_accessed=8 << 20, transcendentals=0),
    )(w, bias)


def decode(terms, packed, tr, tc):
    bins = terms.shape[0]
    ch = packed[2].shape[0]
    f32, bf16 = jnp.float32, jnp.bfloat16
    vm = pl.BlockSpec(memory_space=pltpu.VMEM)
    wide, span = tc + 16, tc + 8
    pairs0, groups1 = (tr + 12) // 2, (tr + 8) // 4
    tall = -(-(tr + 12) // 8) * 8
    scratch = (
        ((bins + 2 * PAD, LANES), f32),
        ((bins + 2 * PAD, LANES), f32),
        ((2, 3, wide + 8, LANES), f32),
        ((2, 3, tall, LANES), f32),
        ((2, wide + 8, LANES), f32),
        ((2, tall, LANES), f32),
        ((2, 2, pairs0 // 2 + 1, 3, wide, LANES), f32),
        ((4, groups1 // 2 + 1, 3, span, LANES), f32),
        ((ch * tr, LANES), f32),
    )
    return pl.pallas_call(
        functools.partial(decoder_kernel, tr, tc),
        out_shape=jax.ShapeDtypeStruct((ch, tr, tc), bf16),
        in_specs=[vm] * 4,
        out_specs=vm,
        scratch_shapes=[pltpu.VMEM(*s) for s in scratch],
        compiler_params=pltpu.CompilerParams(vmem_limit_bytes=DECODE_BYTES),
    )(terms, *packed)


def project_kernel(bins_hbm, row_hbm, col_hbm, send_ref, bins, w, sems):
    ch = row_hbm.shape[0]
    copies = [
        pltpu.make_async_copy(row_hbm, w.at[0:ch], sems.at[0]),
        pltpu.make_async_copy(col_hbm, w.at[LANES:LANES + ch], sems.at[1]),
        pltpu.make_async_copy(bins_hbm, bins, sems.at[2]),
    ]
    for copy in copies:
        copy.start()
    for p in range(2):
        w[p * LANES + ch:(p + 1) * LANES] = jnp.zeros((LANES - ch, w.shape[1]), w.dtype)
    for copy in copies:
        copy.wait()
    both = lax.dot_general(bins[...], w[...], NT, preferred_element_type=jnp.float32)
    both = both.astype(send_ref.dtype)
    for k in range(send_ref.shape[0]):
        send_ref[k] = both


def project(bins, row_proj, col_proj, peers):
    return pl.pallas_call(
        project_kernel,
        out_shape=jax.ShapeDtypeStruct((peers, bins.shape[0], 2 * LANES), jnp.bfloat16),
        in_specs=[pl.BlockSpec(memory_space=pltpu.HBM)] * 3,
        out_specs=pl.BlockSpec(memory_space=pltpu.VMEM),
        scratch_shapes=[
            pltpu.VMEM(bins.shape, bins.dtype),
            pltpu.VMEM((2 * LANES, bins.shape[1]), bins.dtype),
            pltpu.SemaphoreType.DMA((3,)),
        ],
    )(bins, row_proj, col_proj)


def shards(bins, row_proj, col_proj, conv_weight, conv_bias):
    rows = lax.axis_size("row")
    cols = lax.axis_size("col")
    reps = lax.axis_size("rep")
    part = conv_bias.shape[1]
    if reps > 1:
        row_proj = lax.all_gather(row_proj, "rep", axis=0, tiled=True)
        col_proj = lax.all_gather(col_proj, "rep", axis=0, tiled=True)
        conv_weight = lax.all_gather(conv_weight, "rep", axis=2, tiled=True)
        conv_bias = lax.all_gather(conv_bias, "rep", axis=1, tiled=True)
    peers = rows * cols
    total = bins.shape[0] * peers
    send = project(bins, row_proj, col_proj, peers)
    terms = lax.all_to_all(send, ("row", "col"), 0, 0, tiled=True)
    terms = terms.reshape(total, 2 * LANES)
    packed = filters(conv_weight, conv_bias)
    out = decode(terms, packed, total // rows, total // cols)
    if reps > 1:
        out = lax.dynamic_slice_in_dim(out, lax.axis_index("rep") * part, part, 0)
    return out


def solution(mesh):
    placed = (
        P(("groups", "row", "col"), None),
        P("rep", None),
        P("rep", None),
        P(None, None, "rep", None),
        P(None, "rep"),
    )
    return jax.shard_map(
        shards,
        mesh=mesh,
        in_specs=placed,
        out_specs=P("rep", ("groups", "row"), "col"),
        check_vma=False,
    )
```

```python
import functools
import jax
import jax.numpy as jnp
from jax import lax
from jax.experimental import pallas as pl
from jax.experimental.pallas import tpu as pltpu
from jax.sharding import PartitionSpec as P

LANES = 128
PAD = 16
BLOCKS = 9
STEP0 = 4
STEP1 = 1
STEP2 = 1
APART = True
WIDTH = BLOCKS * LANES
LAST = 4 * WIDTH
PACKED = LAST + WIDTH + 2 * LANES
FRONT_BYTES = 48 << 20
DECODE_BYTES = 40 << 20
NT = (((1,), (1,)), ((), ()))


def cuts(count, most):
    parts = -(-count // most)
    edges = [count * k // parts for k in range(parts + 1)]
    return list(zip(edges[:-1], edges[1:]))


def lane_ids(shape):
    return lax.broadcasted_iota(jnp.int32, shape, len(shape) - 1)


def third_of(value, ch, t):
    spare = LANES - ch
    return pltpu.roll(value, (ch - t * spare) % LANES, value.ndim - 1)


def filters_kernel(w_ref, b_ref, packed, bias_ref, column_ref, wide):
    ch = w_ref.shape[2]
    spare = LANES - ch
    f32, bf16 = jnp.float32, jnp.bfloat16
    wide[...] = jnp.zeros(wide.shape, f32)

    def fill(rows0, rows1, first, layer, swap):
        for b in range(3):
            taps = []
            for a in range(3):
                wide[:, 0:ch] = w_ref[layer, 3 * b + a if swap else 3 * a + b].astype(f32)
                taps.append(wide[...])
            for t in range(3):
                cols = slice(first + (3 * t + b) * LANES, first + (3 * t + b + 1) * LANES)
                packed[rows0, cols] = taps[t].astype(bf16)
                main = taps[t - 1] if t else jnp.zeros((ch, LANES), f32)
                moved = third_of(taps[2], ch, t)
                packed[rows1, cols] = jnp.where(lane_ids((ch, LANES)) < ch, main, moved).astype(bf16)

    low, high = slice(0, ch), slice(LANES, LANES + ch)
    for p in range(2):
        packed[p * LANES + ch:(p + 1) * LANES, 0:LAST] = jnp.zeros((spare, LAST), bf16)
    for layer in range(2):
        fill(low, high, 2 * layer * WIDTH, layer, False)
        fill(low, high, (2 * layer + 1) * WIDTH, layer, True)
    fill(slice(0, ch), slice(ch, 2 * ch), LAST, 2, False)
    eye = lax.broadcasted_iota(jnp.int32, (ch, LANES), 0) == lane_ids((ch, LANES))
    unit = jnp.where(eye, 1.0, 0.0)
    for p in range(2):
        for s in range(2):
            part = unit if p == s else jnp.zeros((ch, LANES), f32)
            packed[p * ch:(p + 1) * ch, PACKED - (2 - s) * LANES:PACKED - (1 - s) * LANES] = part.astype(bf16)
    blank = jnp.zeros((b_ref.shape[0], spare), f32)
    bias = jnp.concatenate([b_ref[...], blank], axis=1)
    bias_ref[...] = bias
    column_ref[...] = jnp.broadcast_to(
        jnp.sum(unit * bias[2:3, :], axis=1, keepdims=True), (ch, LANES))


def decoder_kernel(tr, tc, terms_ref, packed, bias_ref, column_ref, out_ref,
                   rows_f, cols_f, mixed_v, mixed_u, plain_v, plain_u, h1, sym, acc):
    bins = terms_ref.shape[0] * terms_ref.shape[2] * 2
    ch = out_ref.shape[0]
    wide = tc + 16
    span = tc + 8
    f32, bf16 = jnp.float32, jnp.bfloat16
    i0 = lax.axis_index("row") * tr
    j0 = lax.axis_index("col") * tc
    top, bottom = i0 == 0, i0 + tr == bins
    left, right = j0 == 0, j0 + tc == bins
    bias0 = bias_ref[0:1, :]
    bias1 = bias_ref[1:2, :]

    def stage(body):
        if APART:
            pl.when(i0 >= 0)(body)
        else:
            body()

    peers, _, half, _ = terms_ref.shape
    for tab in (rows_f, cols_f):
        tab[0:PAD] = jnp.zeros((PAD, LANES), f32)
        tab[PAD + bins:] = jnp.zeros((PAD, LANES), f32)
    for s in range(peers):
        rest = terms_ref[s, 2].astype(f32)
        for i in range(2):
            at = PAD + (2 * s + i) * half
            rows_f[at:at + half] = terms_ref[s, i].astype(f32)
            cols_f[at:at + half] = rest
    spare = LANES - ch
    shape = (bins, LANES)
    rest = cols_f[PAD:PAD + bins]
    early = lax.rem(lax.broadcasted_iota(jnp.int32, shape, 0), 2 * half) < half
    rest = jnp.where(early, pltpu.roll(rest, spare, 1), pltpu.roll(rest, ch, 1))
    cols_f[PAD:PAD + bins] = jnp.where(
        lane_ids(shape) < spare, pltpu.roll(rows_f[PAD:PAD + bins], spare, 1), rest)

    pairs0 = (tr + 12) // 2
    tall = mixed_u.shape[2]
    body_v = lane_ids((wide + 8, LANES)) < ch
    body_u = lane_ids((tall, LANES)) < ch
    for m, (u_src, v_src) in enumerate(((rows_f, cols_f), (cols_f, rows_f))):
        line = v_src[pl.ds(j0 + PAD - 9, wide + 8), :]
        plain_v[m] = line
        for t in range(3):
            mixed_v[m, t] = jnp.where(body_v, line, third_of(line, ch, t))
        fourth = u_src[pl.ds(i0 + PAD - 7 + 3, tall), :]
        for t in range(3):
            row = u_src[pl.ds(i0 + PAD - 7 + t, tall), :]
            mixed_u[m, t] = jnp.where(body_u, row, third_of(fourth, ch, t))
        plain_u[m] = u_src[pl.ds(i0 + PAD - 6, tall), :]

    def put(ref, where, k, value, width):
        at = k // 2 + 1
        cells = slice(0, width)
        if k % 2 == 0:
            ref[where + (at, 0, cells, slice(0, ch))] = value[:, 0:ch]
            ref[where + (at - 1, 2, cells, slice(0, ch))] = value[:, 0:ch]
        else:
            ref[where + (at, 1, cells, slice(0, ch))] = value[:, 0:ch]
            for t in range(3):
                ref[where + (at - 1, t, cells, slice(ch, LANES))] = third_of(value, ch, t)[:, ch:LANES]

    def clear(ref, heads, groups, width, side, deep):
        main, rest = slice(0, ch), slice(ch, LANES)
        body = jnp.zeros((width, ch), f32)
        tail = jnp.zeros((width, LANES - ch), f32)
        edge = jnp.zeros((side, LANES), f32)
        above = [(1, 0, main)] + ([(1, 1, main), (2, 0, main), (1, 2, main)] if deep == 3 else [])
        below = [(groups, t, rest) for t in range(3)]
        if deep == 3:
            below += [(groups, 1, main), (groups, 2, main)] + [(groups - 1, t, rest) for t in range(3)]
        for flag, places in ((top, above), (bottom, below)):
            @pl.when(flag)
            def _(places=places):
                for head in heads:
                    for at, t, lanes in places:
                        ref[head + (at, t, slice(0, width), lanes)] = body if lanes == main else tail
        for flag, start in ((left, 0), (right, width - side)):
            @pl.when(flag)
            def _(start=start):
                for head in heads:
                    for at in range(1, groups + 1):
                        for t in range(3):
                            ref[head + (at, t, slice(start, start + side), slice(0, LANES))] = edge

    def first(m, lo, hi):
        rows = []
        for n in range(lo, hi):
            line = []
            for t in range(3):
                u = jnp.broadcast_to(mixed_u[m, t, 2 * n:2 * n + 1, :], (wide, LANES)).astype(bf16)
                for b in range(3):
                    v = mixed_v[m, t, b:b + wide, :].astype(bf16)
                    line.append(jnp.maximum(v * u, 0))
            rows.append(jnp.concatenate(line, axis=1))
        y = lax.dot_general(jnp.concatenate(rows, axis=0), packed[:, m * WIDTH:(m + 1) * WIDTH], NT,
                            preferred_element_type=f32)
        for k, n in enumerate(range(lo, hi)):
            for e in range(2):
                own = plain_v[m, 1:1 + wide, :] * plain_u[m, 2 * n + e:2 * n + e + 1, :]
                part = y[k * wide:(k + 1) * wide, e * LANES:(e + 1) * LANES]
                put(h1, (m, e), n, part + own + bias0, wide)

    for m in range(2):
        for lo, hi in cuts(pairs0, STEP0):
            stage(functools.partial(first, m, lo, hi))
    groups1 = (tr + 8) // 4
    clear(h1, [(m, e) for m in range(2) for e in range(2)], groups1, wide, 8, 3)

    def second(lo, hi):
        spots = [(k, e) for k in range(lo, hi) for e in range(2)]
        lhs = []
        for m in range(2):
            for t in range(3):
                for b in range(3):
                    cut = jnp.concatenate([
                        h1[m, e, k + 1, t, 2 + 2 * b:2 + 2 * b + span, :] for k, e in spots], axis=0)
                    lhs.append(jnp.maximum(cut.astype(bf16), 0))
        y = lax.dot_general(jnp.concatenate(lhs, axis=1), packed[:, 2 * WIDTH:LAST], NT, preferred_element_type=f32)
        for s, (k, e) in enumerate(spots):
            for p in range(2):
                both = h1[0, e, k + 1, 1 + p, 4:4 + span, :] + h1[1, e, k + 1, 1 + p, 4:4 + span, :]
                part = y[s * span:(s + 1) * span, p * LANES:(p + 1) * LANES]
                put(sym, (e + 2 * p,), k, (part + both) * 0.5 + bias1, span)

    for lo, hi in cuts(groups1, STEP1):
        stage(functools.partial(second, lo, hi))
    groups2 = tr // 8
    clear(sym, [(e,) for e in range(4)], groups2, span, 4, 1)

    bias2 = column_ref[...]
    def third(lo, hi):
        spots = [(g, e) for g in range(lo, hi) for e in range(4)]
        cells = []
        for g, e in spots:
            line = []
            for t in range(3):
                for b in range(3):
                    line.append(jnp.maximum(sym[e, g + 1, t, 4 * b:4 * b + tc, :].astype(bf16), 0))
            for p in range(2):
                line.append(sym[e, g + 1, 1 + p, 4:4 + tc, :].astype(bf16))
            cells.append(jnp.concatenate(line, axis=1))
        y = lax.dot_general(packed[0:2 * ch, LAST:PACKED], jnp.concatenate(cells, axis=0), NT, preferred_element_type=f32)
        for s, (g, e) in enumerate(spots):
            for p in range(2):
                part = y[p * ch:(p + 1) * ch, s * tc:(s + 1) * tc]
                acc[pl.ds(8 * g + e + 4 * p, ch, stride=tr), :] = part + bias2

    for lo, hi in cuts(groups2, STEP2):
        stage(functools.partial(third, lo, hi))
    out_ref[...] = acc[...].reshape(ch, tr, tc).astype(out_ref.dtype)


def filters(w, bias):
    ch = w.shape[2]
    f32, bf16 = jnp.float32, jnp.bfloat16
    vm = pl.BlockSpec(memory_space=pltpu.VMEM)
    shapes = (
        ((2 * LANES, PACKED), bf16),
        ((bias.shape[0], LANES), f32),
        ((ch, LANES), f32),
    )
    return pl.pallas_call(
        filters_kernel,
        out_shape=[jax.ShapeDtypeStruct(*s) for s in shapes],
        in_specs=[vm, vm],
        out_specs=[vm] * len(shapes),
        scratch_shapes=[pltpu.VMEM((ch, LANES), f32)],
        compiler_params=pltpu.CompilerParams(vmem_limit_bytes=FRONT_BYTES),
        cost_estimate=pl.CostEstimate(flops=0, bytes_accessed=8 << 20, transcendentals=0),
    )(w, bias)


def decode(terms, packed, tr, tc):
    bins = terms.shape[0] * terms.shape[2] * 2
    ch = packed[2].shape[0]
    f32, bf16 = jnp.float32, jnp.bfloat16
    vm = pl.BlockSpec(memory_space=pltpu.VMEM)
    wide, span = tc + 16, tc + 8
    pairs0, groups1 = (tr + 12) // 2, (tr + 8) // 4
    tall = -(-(tr + 12) // 8) * 8
    scratch = (
        ((bins + 2 * PAD, LANES), f32),
        ((bins + 2 * PAD, LANES), f32),
        ((2, 3, wide + 8, LANES), f32),
        ((2, 3, tall, LANES), f32),
        ((2, wide + 8, LANES), f32),
        ((2, tall, LANES), f32),
        ((2, 2, pairs0 // 2 + 1, 3, wide, LANES), f32),
        ((4, groups1 // 2 + 1, 3, span, LANES), f32),
        ((ch * tr, LANES), f32),
    )
    return pl.pallas_call(
        functools.partial(decoder_kernel, tr, tc),
        out_shape=jax.ShapeDtypeStruct((ch, tr, tc), bf16),
        in_specs=[vm] * 4,
        out_specs=vm,
        scratch_shapes=[pltpu.VMEM(*s) for s in scratch],
        compiler_params=pltpu.CompilerParams(vmem_limit_bytes=DECODE_BYTES),
    )(terms, *packed)


def project_kernel(bins_hbm, row_hbm, col_hbm, send_ref, bins, w, sems):
    ch = row_hbm.shape[0]
    half = bins.shape[0] // 2
    copies = [
        pltpu.make_async_copy(bins_hbm, bins, sems.at[0]),
        pltpu.make_async_copy(row_hbm, w.at[0:ch], sems.at[1]),
        pltpu.make_async_copy(col_hbm, w.at[ch:2 * ch], sems.at[2]),
    ]
    for copy in copies:
        copy.start()
    for copy in copies:
        copy.wait()
    both = lax.dot_general(bins[...], w[...], NT, preferred_element_type=jnp.float32)
    full, rest = both[:, 0:LANES], both[:, LANES:]
    rest = jnp.concatenate([rest[0:half], rest[half:]], axis=1)
    for i, part in enumerate((full[0:half], full[half:], rest)):
        part = part.astype(send_ref.dtype)
        for k in range(send_ref.shape[0]):
            send_ref[k, i] = part


def project(bins, row_proj, col_proj, peers):
    span = bins.shape[0]
    return pl.pallas_call(
        project_kernel,
        out_shape=jax.ShapeDtypeStruct((peers, 3, span // 2, LANES), jnp.bfloat16),
        in_specs=[pl.BlockSpec(memory_space=pltpu.HBM)] * 3,
        out_specs=pl.BlockSpec(memory_space=pltpu.VMEM),
        scratch_shapes=[
            pltpu.VMEM(bins.shape, bins.dtype),
            pltpu.VMEM((2 * row_proj.shape[0], bins.shape[1]), bins.dtype),
            pltpu.SemaphoreType.DMA((3,)),
        ],
    )(bins, row_proj, col_proj)


def shards(bins, row_proj, col_proj, conv_weight, conv_bias):
    rows = lax.axis_size("row")
    cols = lax.axis_size("col")
    reps = lax.axis_size("rep")
    part = conv_bias.shape[1]
    if reps > 1:
        row_proj = lax.all_gather(row_proj, "rep", axis=0, tiled=True)
        col_proj = lax.all_gather(col_proj, "rep", axis=0, tiled=True)
        conv_weight = lax.all_gather(conv_weight, "rep", axis=2, tiled=True)
        conv_bias = lax.all_gather(conv_bias, "rep", axis=1, tiled=True)
    peers = rows * cols
    total = bins.shape[0] * peers
    send = project(bins, row_proj, col_proj, peers)
    terms = lax.all_to_all(send, ("row", "col"), 0, 0, tiled=True)
    packed = filters(conv_weight, conv_bias)
    out = decode(terms, packed, total // rows, total // cols)
    if reps > 1:
        out = lax.dynamic_slice_in_dim(out, lax.axis_index("rep") * part, part, 0)
    return out


def solution(mesh):
    placed = (
        P(("groups", "row", "col"), None),
        P("rep", None),
        P("rep", None),
        P(None, None, "rep", None),
        P(None, "rep"),
    )
    return jax.shard_map(
        shards,
        mesh=mesh,
        in_specs=placed,
        out_specs=P("rep", ("groups", "row"), "col"),
        check_vma=False,
    )
```

```python
import functools
import jax
import jax.numpy as jnp
from jax import lax
from jax.experimental import pallas as pl
from jax.experimental.pallas import tpu as pltpu
from jax.sharding import PartitionSpec as P

LANES = 128
PAD = 16
BLOCKS = 9
STEP0 = 4
STEP1 = 1
STEP2 = 1
APART = True
WIDTH = BLOCKS * LANES
LAST = 4 * WIDTH
PACKED = LAST + WIDTH + 2 * LANES
FRONT_BYTES = 48 << 20
DECODE_BYTES = 40 << 20
NT = (((1,), (1,)), ((), ()))


def cuts(count, most):
    parts = -(-count // most)
    edges = [count * k // parts for k in range(parts + 1)]
    return list(zip(edges[:-1], edges[1:]))


def lane_ids(shape):
    return lax.broadcasted_iota(jnp.int32, shape, len(shape) - 1)


def third_of(value, ch, t):
    spare = LANES - ch
    return pltpu.roll(value, (ch - t * spare) % LANES, value.ndim - 1)


def filters_kernel(w_ref, b_ref, packed, bias_ref, column_ref, wide):
    ch = w_ref.shape[2]
    spare = LANES - ch
    f32, bf16 = jnp.float32, jnp.bfloat16
    wide[...] = jnp.zeros(wide.shape, f32)

    def fill(rows0, rows1, first, layer, swap):
        for b in range(3):
            taps = []
            for a in range(3):
                wide[:, 0:ch] = w_ref[layer, 3 * b + a if swap else 3 * a + b].astype(f32)
                taps.append(wide[...])
            for t in range(3):
                cols = slice(first + (3 * t + b) * LANES, first + (3 * t + b + 1) * LANES)
                packed[rows0, cols] = taps[t].astype(bf16)
                main = taps[t - 1] if t else jnp.zeros((ch, LANES), f32)
                moved = third_of(taps[2], ch, t)
                packed[rows1, cols] = jnp.where(lane_ids((ch, LANES)) < ch, main, moved).astype(bf16)

    low, high = slice(0, ch), slice(LANES, LANES + ch)
    for p in range(2):
        packed[p * LANES + ch:(p + 1) * LANES, 0:LAST] = jnp.zeros((spare, LAST), bf16)
    for layer in range(2):
        fill(low, high, 2 * layer * WIDTH, layer, False)
        fill(low, high, (2 * layer + 1) * WIDTH, layer, True)
    fill(slice(0, ch), slice(ch, 2 * ch), LAST, 2, False)
    eye = lax.broadcasted_iota(jnp.int32, (ch, LANES), 0) == lane_ids((ch, LANES))
    unit = jnp.where(eye, 1.0, 0.0)
    for p in range(2):
        for s in range(2):
            part = unit if p == s else jnp.zeros((ch, LANES), f32)
            packed[p * ch:(p + 1) * ch, PACKED - (2 - s) * LANES:PACKED - (1 - s) * LANES] = part.astype(bf16)
    blank = jnp.zeros((b_ref.shape[0], spare), f32)
    bias = jnp.concatenate([b_ref[...], blank], axis=1)
    bias_ref[...] = bias
    column_ref[...] = jnp.broadcast_to(
        jnp.sum(unit * bias[2:3, :], axis=1, keepdims=True), (ch, LANES))


def decoder_kernel(tr, tc, terms_ref, packed, bias_ref, column_ref, out_ref,
                   rows_f, cols_f, mixed_v, mixed_u, plain_v, plain_u, h1, sym, acc):
    bins = terms_ref.shape[0] * terms_ref.shape[2] * 2
    ch = out_ref.shape[0]
    wide = tc + 16
    span = tc + 8
    f32, bf16 = jnp.float32, jnp.bfloat16
    i0 = lax.axis_index("row") * tr
    j0 = lax.axis_index("col") * tc
    top, bottom = i0 == 0, i0 + tr == bins
    left, right = j0 == 0, j0 + tc == bins
    bias0 = bias_ref[0:1, :]
    bias1 = bias_ref[1:2, :]

    def stage(body):
        if APART:
            pl.when(i0 >= 0)(body)
        else:
            body()

    peers, _, half, _ = terms_ref.shape
    for tab in (rows_f, cols_f):
        tab[0:PAD] = jnp.zeros((PAD, LANES), f32)
        tab[PAD + bins:] = jnp.zeros((PAD, LANES), f32)
    for s in range(peers):
        rest = terms_ref[s, 2].astype(f32)
        for i in range(2):
            at = PAD + (2 * s + i) * half
            rows_f[at:at + half] = terms_ref[s, i].astype(f32)
            cols_f[at:at + half] = rest
    spare = LANES - ch
    shape = (bins, LANES)
    rest = cols_f[PAD:PAD + bins]
    early = lax.rem(lax.broadcasted_iota(jnp.int32, shape, 0), 2 * half) < half
    rest = jnp.where(early, pltpu.roll(rest, spare, 1), pltpu.roll(rest, ch, 1))
    cols_f[PAD:PAD + bins] = jnp.where(
        lane_ids(shape) < spare, pltpu.roll(rows_f[PAD:PAD + bins], spare, 1), rest)

    pairs0 = (tr + 12) // 2
    tall = mixed_u.shape[2]
    body_v = lane_ids((wide + 8, LANES)) < ch
    body_u = lane_ids((tall, LANES)) < ch
    for m, (u_src, v_src) in enumerate(((rows_f, cols_f), (cols_f, rows_f))):
        line = v_src[pl.ds(j0 + PAD - 9, wide + 8), :]
        plain_v[m] = line
        for t in range(3):
            mixed_v[m, t] = jnp.where(body_v, line, third_of(line, ch, t))
        fourth = u_src[pl.ds(i0 + PAD - 7 + 3, tall), :]
        for t in range(3):
            row = u_src[pl.ds(i0 + PAD - 7 + t, tall), :]
            mixed_u[m, t] = jnp.where(body_u, row, third_of(fourth, ch, t))
        plain_u[m] = u_src[pl.ds(i0 + PAD - 6, tall), :]

    def put(ref, where, k, value, width):
        at = k // 2 + 1
        cells = slice(0, width)
        if k % 2 == 0:
            ref[where + (at, 0, cells, slice(0, ch))] = value[:, 0:ch]
            ref[where + (at - 1, 2, cells, slice(0, ch))] = value[:, 0:ch]
        else:
            ref[where + (at, 1, cells, slice(0, ch))] = value[:, 0:ch]
            for t in range(3):
                ref[where + (at - 1, t, cells, slice(ch, LANES))] = third_of(value, ch, t)[:, ch:LANES]

    def kept(outside):
        return jnp.where(outside, 0.0, 1.0).astype(f32)

    keep_top, keep_bottom = kept(top), kept(bottom)
    sub = lax.broadcasted_iota(jnp.int32, (8, LANES), 0)
    sides0 = (jnp.full((8, LANES), kept(left)), jnp.full((8, LANES), kept(right)))
    sides1 = (jnp.where((sub < 4) & left, 0.0, 1.0), jnp.where((sub >= 4) & right, 0.0, 1.0))

    def inside(value, sides, above, below):
        width = value.shape[0]
        value = jnp.concatenate([
            value[0:8] * sides[0], value[8:width - 8], value[width - 8:] * sides[1]], axis=0)
        if above:
            value = value * keep_top
        if below:
            value = value * keep_bottom
        return value

    def first(m, lo, hi):
        rows = []
        for n in range(lo, hi):
            line = []
            for t in range(3):
                u = jnp.broadcast_to(mixed_u[m, t, 2 * n:2 * n + 1, :], (wide, LANES)).astype(bf16)
                for b in range(3):
                    v = mixed_v[m, t, b:b + wide, :].astype(bf16)
                    line.append(jnp.maximum(v * u, 0))
            rows.append(jnp.concatenate(line, axis=1))
        y = lax.dot_general(jnp.concatenate(rows, axis=0), packed[:, m * WIDTH:(m + 1) * WIDTH], NT,
                            preferred_element_type=f32)
        for k, n in enumerate(range(lo, hi)):
            for e in range(2):
                own = plain_v[m, 1:1 + wide, :] * plain_u[m, 2 * n + e:2 * n + e + 1, :]
                part = y[k * wide:(k + 1) * wide, e * LANES:(e + 1) * LANES]
                value = inside(part + own + bias0, sides0, n < 3, n >= pairs0 - 3)
                put(h1, (m, e), n, value, wide)

    for m in range(2):
        for lo, hi in cuts(pairs0, STEP0):
            stage(functools.partial(first, m, lo, hi))
    groups1 = (tr + 8) // 4

    def second(lo, hi):
        spots = [(k, e) for k in range(lo, hi) for e in range(2)]
        lhs = []
        for m in range(2):
            for t in range(3):
                for b in range(3):
                    cut = jnp.concatenate([
                        h1[m, e, k + 1, t, 2 + 2 * b:2 + 2 * b + span, :] for k, e in spots], axis=0)
                    lhs.append(jnp.maximum(cut.astype(bf16), 0))
        y = lax.dot_general(jnp.concatenate(lhs, axis=1), packed[:, 2 * WIDTH:LAST], NT, preferred_element_type=f32)
        for s, (k, e) in enumerate(spots):
            for p in range(2):
                both = h1[0, e, k + 1, 1 + p, 4:4 + span, :] + h1[1, e, k + 1, 1 + p, 4:4 + span, :]
                part = y[s * span:(s + 1) * span, p * LANES:(p + 1) * LANES]
                value = inside((part + both) * 0.5 + bias1, sides1, k < 1, k >= groups1 - 1)
                put(sym, (e + 2 * p,), k, value, span)

    for lo, hi in cuts(groups1, STEP1):
        stage(functools.partial(second, lo, hi))
    groups2 = tr // 8

    bias2 = column_ref[...]
    def third(lo, hi):
        spots = [(g, e) for g in range(lo, hi) for e in range(4)]
        cells = []
        for g, e in spots:
            line = []
            for t in range(3):
                for b in range(3):
                    line.append(jnp.maximum(sym[e, g + 1, t, 4 * b:4 * b + tc, :].astype(bf16), 0))
            for p in range(2):
                line.append(sym[e, g + 1, 1 + p, 4:4 + tc, :].astype(bf16))
            cells.append(jnp.concatenate(line, axis=1))
        y = lax.dot_general(packed[0:2 * ch, LAST:PACKED], jnp.concatenate(cells, axis=0), NT, preferred_element_type=f32)
        for s, (g, e) in enumerate(spots):
            for p in range(2):
                part = y[p * ch:(p + 1) * ch, s * tc:(s + 1) * tc]
                acc[pl.ds(8 * g + e + 4 * p, ch, stride=tr), :] = part + bias2

    for lo, hi in cuts(groups2, STEP2):
        stage(functools.partial(third, lo, hi))
    out_ref[...] = acc[...].reshape(ch, tr, tc).astype(out_ref.dtype)


def filters(w, bias):
    ch = w.shape[2]
    f32, bf16 = jnp.float32, jnp.bfloat16
    vm = pl.BlockSpec(memory_space=pltpu.VMEM)
    shapes = (
        ((2 * LANES, PACKED), bf16),
        ((bias.shape[0], LANES), f32),
        ((ch, LANES), f32),
    )
    return pl.pallas_call(
        filters_kernel,
        out_shape=[jax.ShapeDtypeStruct(*s) for s in shapes],
        in_specs=[vm, vm],
        out_specs=[vm] * len(shapes),
        scratch_shapes=[pltpu.VMEM((ch, LANES), f32)],
        compiler_params=pltpu.CompilerParams(vmem_limit_bytes=FRONT_BYTES),
        cost_estimate=pl.CostEstimate(flops=0, bytes_accessed=8 << 20, transcendentals=0),
    )(w, bias)


def decode(terms, packed, tr, tc):
    bins = terms.shape[0] * terms.shape[2] * 2
    ch = packed[2].shape[0]
    f32, bf16 = jnp.float32, jnp.bfloat16
    vm = pl.BlockSpec(memory_space=pltpu.VMEM)
    wide, span = tc + 16, tc + 8
    pairs0, groups1 = (tr + 12) // 2, (tr + 8) // 4
    tall = -(-(tr + 12) // 8) * 8
    scratch = (
        ((bins + 2 * PAD, LANES), f32),
        ((bins + 2 * PAD, LANES), f32),
        ((2, 3, wide + 8, LANES), f32),
        ((2, 3, tall, LANES), f32),
        ((2, wide + 8, LANES), f32),
        ((2, tall, LANES), f32),
        ((2, 2, pairs0 // 2 + 1, 3, wide, LANES), f32),
        ((4, groups1 // 2 + 1, 3, span, LANES), f32),
        ((ch * tr, LANES), f32),
    )
    return pl.pallas_call(
        functools.partial(decoder_kernel, tr, tc),
        out_shape=jax.ShapeDtypeStruct((ch, tr, tc), bf16),
        in_specs=[vm] * 4,
        out_specs=vm,
        scratch_shapes=[pltpu.VMEM(*s) for s in scratch],
        compiler_params=pltpu.CompilerParams(vmem_limit_bytes=DECODE_BYTES),
    )(terms, *packed)


def project_kernel(bins_hbm, row_hbm, col_hbm, send_ref, bins, w, sems):
    ch = row_hbm.shape[0]
    half = bins.shape[0] // 2
    copies = [
        pltpu.make_async_copy(bins_hbm, bins, sems.at[0]),
        pltpu.make_async_copy(row_hbm, w.at[0:ch], sems.at[1]),
        pltpu.make_async_copy(col_hbm, w.at[ch:2 * ch], sems.at[2]),
    ]
    for copy in copies:
        copy.start()
    for copy in copies:
        copy.wait()
    both = lax.dot_general(bins[...], w[...], NT, preferred_element_type=jnp.float32)
    full, rest = both[:, 0:LANES], both[:, LANES:]
    rest = jnp.concatenate([rest[0:half], rest[half:]], axis=1)
    for i, part in enumerate((full[0:half], full[half:], rest)):
        part = part.astype(send_ref.dtype)
        for k in range(send_ref.shape[0]):
            send_ref[k, i] = part


def project(bins, row_proj, col_proj, peers):
    span = bins.shape[0]
    return pl.pallas_call(
        project_kernel,
        out_shape=jax.ShapeDtypeStruct((peers, 3, span // 2, LANES), jnp.bfloat16),
        in_specs=[pl.BlockSpec(memory_space=pltpu.HBM)] * 3,
        out_specs=pl.BlockSpec(memory_space=pltpu.VMEM),
        scratch_shapes=[
            pltpu.VMEM(bins.shape, bins.dtype),
            pltpu.VMEM((2 * row_proj.shape[0], bins.shape[1]), bins.dtype),
            pltpu.SemaphoreType.DMA((3,)),
        ],
    )(bins, row_proj, col_proj)


def shards(bins, row_proj, col_proj, conv_weight, conv_bias):
    rows = lax.axis_size("row")
    cols = lax.axis_size("col")
    reps = lax.axis_size("rep")
    part = conv_bias.shape[1]
    if reps > 1:
        row_proj = lax.all_gather(row_proj, "rep", axis=0, tiled=True)
        col_proj = lax.all_gather(col_proj, "rep", axis=0, tiled=True)
        conv_weight = lax.all_gather(conv_weight, "rep", axis=2, tiled=True)
        conv_bias = lax.all_gather(conv_bias, "rep", axis=1, tiled=True)
    peers = rows * cols
    total = bins.shape[0] * peers
    send = project(bins, row_proj, col_proj, peers)
    terms = lax.all_to_all(send, ("row", "col"), 0, 0, tiled=True)
    packed = filters(conv_weight, conv_bias)
    out = decode(terms, packed, total // rows, total // cols)
    if reps > 1:
        out = lax.dynamic_slice_in_dim(out, lax.axis_index("rep") * part, part, 0)
    return out


def solution(mesh):
    placed = (
        P(("groups", "row", "col"), None),
        P("rep", None),
        P("rep", None),
        P(None, None, "rep", None),
        P(None, "rep"),
    )
    return jax.shard_map(
        shards,
        mesh=mesh,
        in_specs=placed,
        out_specs=P("rep", ("groups", "row"), "col"),
        check_vma=False,
    )
```

```python
import functools
import jax
import jax.numpy as jnp
from jax import lax
from jax.experimental import pallas as pl
from jax.experimental.pallas import tpu as pltpu
from jax.sharding import PartitionSpec as P

LANES = 128
PAD = 16
BLOCKS = 9
STEP0 = 7
STEP1 = 3
APART = True
BESIDE = True
MIXED = False
WIDTH = BLOCKS * LANES
LAST = 4 * WIDTH
PACKED = LAST + WIDTH + 2 * LANES
FRONT_BYTES = 48 << 20
DECODE_BYTES = 40 << 20
NT = (((1,), (1,)), ((), ()))


def cuts(count, most):
    parts = -(-count // most)
    edges = [count * k // parts for k in range(parts + 1)]
    return list(zip(edges[:-1], edges[1:]))


def lane_ids(shape):
    return lax.broadcasted_iota(jnp.int32, shape, len(shape) - 1)


def third_of(value, ch, t):
    spare = LANES - ch
    return pltpu.roll(value, (ch - t * spare) % LANES, value.ndim - 1)


def filters_kernel(w_ref, b_ref, packed, bias_ref, column_ref, wide):
    ch = w_ref.shape[2]
    spare = LANES - ch
    f32, bf16 = jnp.float32, jnp.bfloat16
    wide[...] = jnp.zeros(wide.shape, f32)

    def fill(rows0, rows1, first, layer, swap):
        for b in range(3):
            taps = []
            for a in range(3):
                wide[:, 0:ch] = w_ref[layer, 3 * b + a if swap else 3 * a + b].astype(f32)
                taps.append(wide[...])
            for t in range(3):
                cols = slice(first + (3 * t + b) * LANES, first + (3 * t + b + 1) * LANES)
                packed[rows0, cols] = taps[t].astype(bf16)
                main = taps[t - 1] if t else jnp.zeros((ch, LANES), f32)
                moved = third_of(taps[2], ch, t)
                packed[rows1, cols] = jnp.where(lane_ids((ch, LANES)) < ch, main, moved).astype(bf16)

    low, high = slice(0, ch), slice(LANES, LANES + ch)
    for p in range(2):
        packed[p * LANES + ch:(p + 1) * LANES, 0:LAST] = jnp.zeros((spare, LAST), bf16)
    for layer in range(2):
        fill(low, high, 2 * layer * WIDTH, layer, False)
        fill(low, high, (2 * layer + 1) * WIDTH, layer, True)
    fill(slice(0, ch), slice(ch, 2 * ch), LAST, 2, False)
    eye = lax.broadcasted_iota(jnp.int32, (ch, LANES), 0) == lane_ids((ch, LANES))
    unit = jnp.where(eye, 1.0, 0.0)
    for p in range(2):
        for s in range(2):
            part = unit if p == s else jnp.zeros((ch, LANES), f32)
            packed[p * ch:(p + 1) * ch, PACKED - (2 - s) * LANES:PACKED - (1 - s) * LANES] = part.astype(bf16)
    blank = jnp.zeros((b_ref.shape[0], spare), f32)
    bias = jnp.concatenate([b_ref[...], blank], axis=1)
    bias_ref[...] = bias
    column_ref[...] = jnp.broadcast_to(
        jnp.sum(unit * bias[2:3, :], axis=1, keepdims=True), (ch, LANES))


def decoder_kernel(tr, tc, terms_ref, packed, bias_ref, column_ref, out_ref,
                   rows_f, cols_f, mixed_v, mixed_u, plain_v, plain_u, h1, sym, acc):
    bins = terms_ref.shape[0] * terms_ref.shape[2] * 2
    ch = out_ref.shape[0]
    wide = tc + 16
    span = tc + 8
    f32, bf16 = jnp.float32, jnp.bfloat16
    i0 = lax.axis_index("row") * tr
    j0 = lax.axis_index("col") * tc
    top, bottom = i0 == 0, i0 + tr == bins
    left, right = j0 == 0, j0 + tc == bins
    bias0 = bias_ref[0:1, :]
    bias1 = bias_ref[1:2, :]

    def stage(body):
        if APART:
            pl.when(i0 < bins)(body)
        else:
            body()

    peers, _, half, _ = terms_ref.shape
    for tab in (rows_f, cols_f):
        tab[0:PAD] = jnp.zeros((PAD, LANES), f32)
        tab[PAD + bins:] = jnp.zeros((PAD, LANES), f32)
    for s in range(peers):
        rest = terms_ref[s, 2].astype(f32)
        for i in range(2):
            at = PAD + (2 * s + i) * half
            rows_f[at:at + half] = terms_ref[s, i].astype(f32)
            cols_f[at:at + half] = rest

    def row_terms(at, count, phase):
        first = rows_f[pl.ds(at, count), :]
        return first, lambda: [third_of(first, ch, t) for t in range(3)]

    def col_terms(at, count, phase):
        first, rest = rows_f[pl.ds(at, count), :], cols_f[pl.ds(at, count), :]
        shape = (count, LANES)
        early = lax.rem(lax.broadcasted_iota(jnp.int32, shape, 0) + phase, 2 * half) < half
        spare = LANES - ch
        one, three = pltpu.roll(rest, spare, 1), pltpu.roll(rest, ch, 1)
        main = jnp.where(early, one, three)
        main = jnp.where(lane_ids(shape) < spare, pltpu.roll(first, spare, 1), main)
        return main, lambda: [
            first, jnp.where(early, three, one), jnp.where(early, pltpu.roll(rest, 2 * spare, 1), rest)]

    pairs0 = (tr + 12) // 2
    tall = mixed_u.shape[2]
    body_v = lane_ids((wide + 8, LANES)) < ch
    body_u = lane_ids((tall, LANES)) < ch
    for m, (u_terms, v_terms) in enumerate(((row_terms, col_terms), (col_terms, row_terms))):
        _, fourth = u_terms(i0 + PAD - 4, tall, PAD - 4)
        for t, moved in enumerate(fourth()):
            row, _ = u_terms(i0 + PAD - 7 + t, tall, PAD - 7 + t)
            mixed_u[m, t] = jnp.where(body_u, row, moved)
            if t == 1:
                plain_u[m] = row
        line, parts = v_terms(j0 + PAD - 9, wide + 8, PAD - 9)
        plain_v[m] = line
        for t, moved in enumerate(parts()):
            mixed_v[m, t] = jnp.where(body_v, line, moved)

    def put(ref, where, k, value, width):
        at = k // 2 + 1
        cells = slice(0, width)
        if k % 2 == 0:
            ref[where + (at, 0, cells, slice(0, ch))] = value[:, 0:ch]
            ref[where + (at - 1, 2, cells, slice(0, ch))] = value[:, 0:ch]
        else:
            ref[where + (at, 1, cells, slice(0, ch))] = value[:, 0:ch]
            for t in range(3):
                ref[where + (at - 1, t, cells, slice(ch, LANES))] = third_of(value, ch, t)[:, ch:LANES]

    def kept(outside):
        return jnp.where(outside, 0.0, 1.0).astype(f32)

    keep_top, keep_bottom = kept(top), kept(bottom)
    sub = lax.broadcasted_iota(jnp.int32, (8, LANES), 0)
    sides0 = (jnp.full((8, LANES), kept(left)), jnp.full((8, LANES), kept(right)))
    sides1 = (jnp.where((sub < 4) & left, 0.0, 1.0), jnp.where((sub >= 4) & right, 0.0, 1.0))

    def inside(value, sides, above, below):
        width = value.shape[0]
        value = jnp.concatenate([
            value[0:8] * sides[0], value[8:width - 8], value[width - 8:] * sides[1]], axis=0)
        if above:
            value = value * keep_top
        if below:
            value = value * keep_bottom
        return value

    def first(m, lo, hi):
        rows = []
        for n in range(lo, hi):
            line = []
            for t in range(3):
                u = jnp.broadcast_to(mixed_u[m, t, 2 * n:2 * n + 1, :], (wide, LANES)).astype(bf16)
                for b in range(3):
                    v = mixed_v[m, t, b:b + wide, :].astype(bf16)
                    line.append(jnp.maximum(v * u, 0))
            rows.append(jnp.concatenate(line, axis=1))
        y = lax.dot_general(jnp.concatenate(rows, axis=0), packed[:, m * WIDTH:(m + 1) * WIDTH], NT,
                            preferred_element_type=f32)
        for k, n in enumerate(range(lo, hi)):
            for e in range(2):
                own = plain_v[m, 1:1 + wide, :] * plain_u[m, 2 * n + e:2 * n + e + 1, :]
                part = y[k * wide:(k + 1) * wide, e * LANES:(e + 1) * LANES]
                value = inside(part + own + bias0, sides0, n < 3, n >= pairs0 - 3)
                put(h1, (m, e), n, value, wide)

    order = [(m, lo, hi) for lo, hi in cuts(pairs0, STEP0) for m in range(2)]
    if not MIXED:
        order = sorted(order)
    for m, lo, hi in order:
        stage(functools.partial(first, m, lo, hi))
    groups1 = (tr + 8) // 4

    def second(lo, hi):
        spots = [(k, e) for k in range(lo, hi) for e in range(2)]
        lhs = []
        for m in range(2):
            for t in range(3):
                for b in range(3):
                    cut = jnp.concatenate([
                        h1[m, e, k + 1, t, 2 + 2 * b:2 + 2 * b + span, :] for k, e in spots], axis=0)
                    lhs.append(jnp.maximum(cut.astype(bf16), 0))
        y = lax.dot_general(jnp.concatenate(lhs, axis=1), packed[:, 2 * WIDTH:LAST], NT,
                            preferred_element_type=f32)

        def finish():
            for s, (k, e) in enumerate(spots):
                for p in range(2):
                    both = h1[0, e, k + 1, 1 + p, 4:4 + span, :] + h1[1, e, k + 1, 1 + p, 4:4 + span, :]
                    part = y[s * span:(s + 1) * span, p * LANES:(p + 1) * LANES]
                    value = inside((part + both) * 0.5 + bias1, sides1, k < 1, k >= groups1 - 1)
                    put(sym, (e + 2 * p,), k, value, span)
        return finish

    groups2 = tr // 8
    bias2 = column_ref[...]

    def third(g):
        cells = []
        for e in range(4):
            line = []
            for t in range(3):
                for b in range(3):
                    line.append(jnp.maximum(sym[e, g + 1, t, 4 * b:4 * b + tc, :].astype(bf16), 0))
            for p in range(2):
                line.append(sym[e, g + 1, 1 + p, 4:4 + tc, :].astype(bf16))
            cells.append(jnp.concatenate(line, axis=1))
        y = lax.dot_general(packed[0:2 * ch, LAST:PACKED], jnp.concatenate(cells, axis=0), NT,
                            preferred_element_type=f32)

        def finish():
            for e in range(4):
                for p in range(2):
                    part = y[p * ch:(p + 1) * ch, e * tc:(e + 1) * tc]
                    acc[g, pl.ds(e + 4 * p, ch, stride=8), :] = part + bias2
            out_ref[:, 8 * g:8 * g + 8, :] = acc[g].reshape(ch, 8, tc).astype(out_ref.dtype)
        return finish

    def together(makers):
        def body():
            for finish in [make() for make in makers]:
                finish()
        stage(body)

    ready = 0
    for lo, hi in cuts(groups1, STEP1):
        makers = [functools.partial(second, lo, hi)]
        if BESIDE and ready < groups2 and 2 * ready + 4 <= lo and (lo + ready) % 2:
            makers.append(functools.partial(third, ready))
            ready += 1
        together(makers)
    for g in range(ready, groups2):
        together([functools.partial(third, g)])


def filters(w, bias):
    ch = w.shape[2]
    f32, bf16 = jnp.float32, jnp.bfloat16
    vm = pl.BlockSpec(memory_space=pltpu.VMEM)
    shapes = (
        ((2 * LANES, PACKED), bf16),
        ((bias.shape[0], LANES), f32),
        ((ch, LANES), f32),
    )
    return pl.pallas_call(
        filters_kernel,
        out_shape=[jax.ShapeDtypeStruct(*s) for s in shapes],
        in_specs=[vm, vm],
        out_specs=[vm] * len(shapes),
        scratch_shapes=[pltpu.VMEM((ch, LANES), f32)],
        compiler_params=pltpu.CompilerParams(vmem_limit_bytes=FRONT_BYTES),
        cost_estimate=pl.CostEstimate(flops=0, bytes_accessed=8 << 20, transcendentals=0),
    )(w, bias)


def decode(terms, packed, tr, tc):
    bins = terms.shape[0] * terms.shape[2] * 2
    ch = packed[2].shape[0]
    f32, bf16 = jnp.float32, jnp.bfloat16
    vm = pl.BlockSpec(memory_space=pltpu.VMEM)
    wide, span = tc + 16, tc + 8
    pairs0, groups1 = (tr + 12) // 2, (tr + 8) // 4
    tall = -(-(tr + 12) // 8) * 8
    scratch = (
        ((bins + 2 * PAD, LANES), f32),
        ((bins + 2 * PAD, LANES), f32),
        ((2, 3, wide + 8, LANES), f32),
        ((2, 3, tall, LANES), f32),
        ((2, wide + 8, LANES), f32),
        ((2, tall, LANES), f32),
        ((2, 2, pairs0 // 2 + 1, 3, wide, LANES), f32),
        ((4, groups1 // 2 + 1, 3, span, LANES), f32),
        ((tr // 8, ch * 8, LANES), f32),
    )
    return pl.pallas_call(
        functools.partial(decoder_kernel, tr, tc),
        out_shape=jax.ShapeDtypeStruct((ch, tr, tc), bf16),
        in_specs=[vm] * 4,
        out_specs=vm,
        scratch_shapes=[pltpu.VMEM(*s) for s in scratch],
        compiler_params=pltpu.CompilerParams(vmem_limit_bytes=DECODE_BYTES),
    )(terms, *packed)


def project_kernel(bins_hbm, row_hbm, col_hbm, send_ref, bins, w, sems):
    ch = row_hbm.shape[0]
    half = bins.shape[0] // 2
    copies = [
        pltpu.make_async_copy(bins_hbm, bins, sems.at[0]),
        pltpu.make_async_copy(row_hbm, w.at[0:ch], sems.at[1]),
        pltpu.make_async_copy(col_hbm, w.at[ch:2 * ch], sems.at[2]),
    ]
    for copy in copies:
        copy.start()
    for copy in copies:
        copy.wait()
    both = lax.dot_general(bins[...], w[...], NT, preferred_element_type=jnp.float32)
    full, rest = both[:, 0:LANES], both[:, LANES:]
    rest = jnp.concatenate([rest[0:half], rest[half:]], axis=1)
    for i, part in enumerate((full[0:half], full[half:], rest)):
        part = part.astype(send_ref.dtype)
        for k in range(send_ref.shape[0]):
            send_ref[k, i] = part


def project(bins, row_proj, col_proj, peers):
    span = bins.shape[0]
    return pl.pallas_call(
        project_kernel,
        out_shape=jax.ShapeDtypeStruct((peers, 3, span // 2, LANES), jnp.bfloat16),
        in_specs=[pl.BlockSpec(memory_space=pltpu.HBM)] * 3,
        out_specs=pl.BlockSpec(memory_space=pltpu.VMEM),
        scratch_shapes=[
            pltpu.VMEM(bins.shape, bins.dtype),
            pltpu.VMEM((2 * row_proj.shape[0], bins.shape[1]), bins.dtype),
            pltpu.SemaphoreType.DMA((3,)),
        ],
    )(bins, row_proj, col_proj)


def shards(bins, row_proj, col_proj, conv_weight, conv_bias):
    rows = lax.axis_size("row")
    cols = lax.axis_size("col")
    reps = lax.axis_size("rep")
    part = conv_bias.shape[1]
    if reps > 1:
        row_proj = lax.all_gather(row_proj, "rep", axis=0, tiled=True)
        col_proj = lax.all_gather(col_proj, "rep", axis=0, tiled=True)
        conv_weight = lax.all_gather(conv_weight, "rep", axis=2, tiled=True)
        conv_bias = lax.all_gather(conv_bias, "rep", axis=1, tiled=True)
    peers = rows * cols
    total = bins.shape[0] * peers
    send = project(bins, row_proj, col_proj, peers)
    terms = lax.all_to_all(send, ("row", "col"), 0, 0, tiled=True)
    packed = filters(conv_weight, conv_bias)
    out = decode(terms, packed, total // rows, total // cols)
    if reps > 1:
        out = lax.dynamic_slice_in_dim(out, lax.axis_index("rep") * part, part, 0)
    return out


def solution(mesh):
    placed = (
        P(("groups", "row", "col"), None),
        P("rep", None),
        P("rep", None),
        P(None, None, "rep", None),
        P(None, "rep"),
    )
    return jax.shard_map(
        shards,
        mesh=mesh,
        in_specs=placed,
        out_specs=P("rep", ("groups", "row"), "col"),
        check_vma=False,
    )
```
